32 devices in a mesh: task: 2 (over y), fsdp: 8 (over z, x), view: 2 (over core).
Axes of the slice: x: 2, y: 2, z: 4, core: 2. Of those that a mesh axis runs over, the one named last changes fastest.
Arguments:
- train_input: bfloat16 [4, 2048, 8192], P(('task', 'view'), 'fsdp'), parts along dimension 0, may hold values from -6 to 6
- train_query: bfloat16 [4, 2048, 4096], P(('task', 'view'), 'fsdp'), parts along dimension 0, may hold values from -120 to 120, as said below
- train_keys: bfloat16 [4, 2048, 512], P(('task', 'view'), 'fsdp'), parts along dimension 0, may hold values from -6 to 6, as said below
- train_target: bfloat16 [4, 2048, 4096], P(('task', 'view'), 'fsdp'), parts along dimension 0, may hold values from -6 to 6
- train_segments: int32 [4, 8, 256], P(('task', 'view'), 'fsdp'), parts along dimension 0, may hold values from 0 to 7, never falling along the last dimension, each value on 1 to 64 neighbouring positions
- value_weight: bfloat16 [8192, 512], P('fsdp'), may hold values from -0.0625 to 0.0625
- adapter_down: float32 [16384, 64], P(('task', 'fsdp')), parts along dimension 0, may hold values from -0.0625 to 0.0625
- adapter_up: float32 [128, 512], P('task'), parts along dimension 0, may hold values from -0.75 to 0.75
- score_input: bfloat16 [4, 512, 8192], P(('task', 'view'), 'fsdp'), parts along dimension 0, may hold values from -6 to 6
- score_query: bfloat16 [4, 512, 4096], P(('task', 'view'), 'fsdp'), parts along dimension 0, may hold values from -120 to 120, as said below
- score_keys: bfloat16 [4, 512, 512], P(('task', 'view'), 'fsdp'), parts along dimension 0, may hold values from -6 to 6, as said below
- score_segments: int32 [4, 8, 64], P(('task', 'view'), 'fsdp'), parts along dimension 0, may hold values from 0 to 3, never falling along the last dimension, each value on 1 to 32 neighbouring positions
Outputs:
- new_down: float32 [16384, 64], P(('task', 'fsdp')), parts along dimension 0
- new_up: float32 [128, 512], P('task'), parts along dimension 0
- scored: bfloat16 [4, 512, 4096], P(('task', 'view'), 'fsdp'), parts along dimension 0
The draws below stay inside these ranges and needn't reach their ends.
There are 2 independent parts, one for each index of `task`. The reference program is written for one: setup_inputs(seed, part) draws one part's arguments, and reference() takes and returns one part's arrays. A program takes and returns all parts, laid end to end along the dimension named above; an argument that names none is the same for every part. Nothing has to cross between parts.
Inputs may be any that keep to these rules, and one draw needn't show every extreme that they name: `train_query`: query features of each token. `train_keys`: key features of each token. `score_query`: query features of each token. `score_keys`: key features of each token. `train_segments`: ids never decrease along a packed row. `score_segments`: ids never decrease along a packed row.
All inputs are finite; a program needn't handle non-finite values.
Results may differ from the reference program's by a relative error of at most 0.01.
Values may be sent and summed in bfloat16 or wider, within the bound.
No kernel may reach another device: no remote copies, remote signals or barrier semaphores. Data moves between devices by JAX's collectives and lax.ppermute only.
A program may use at most 128 MiB of HBM per device.

```python
import math
import jax
import jax.numpy as jnp
import numpy as np
from jax import lax

D = 8192
Q_HEADS = 32
KV_HEADS = 4
HEAD_DIM = 128
RANK = 64
SEGMENTS = 8
TOK_DEV = 256
SCORE_DEV = 64
VIEWS = 2
GROUP = 8
VALUE_WIDTH = 512
TOKENS = 2048
STOKENS = 512
N_FSDP = 8


def pair_draw(key, rows):
    key_query, key_keys = jax.random.split(key, 2)
    queries = jnp.clip(jax.random.normal(key_query, (VIEWS, rows, Q_HEADS * HEAD_DIM), jnp.float32), -6.0, 6.0)
    keys_all = jnp.clip(jax.random.normal(key_keys, (VIEWS, rows, KV_HEADS * HEAD_DIM), jnp.float32), -6.0, 6.0)
    return (queries, keys_all)


def draw_train_query(key, part):
    return pair_draw(jax.random.fold_in(key, 11), TOKENS)[0].astype(jnp.bfloat16)


def draw_train_keys(key, part):
    return pair_draw(jax.random.fold_in(key, 11), TOKENS)[1].astype(jnp.bfloat16)


def draw_score_query(key, part):
    return pair_draw(jax.random.fold_in(key, 23), STOKENS)[0].astype(jnp.bfloat16)


def draw_score_keys(key, part):
    return pair_draw(jax.random.fold_in(key, 23), STOKENS)[1].astype(jnp.bfloat16)


def with_spikes(entries, rng, source, target, shards_of, factor):
    def block_of(axis_at):
        return (jnp.arange(entries.shape[axis_at]) // (entries.shape[axis_at] // shards_of)).reshape((-1,) + (1,) * (entries.ndim - 1 - axis_at))

    first = jax.random.permutation(rng, shards_of)[block_of(target)]
    other_side = (block_of(target) + shards_of // 2) % shards_of
    return jnp.where((block_of(source) == first) | (block_of(source) == other_side), factor * entries, entries)


def block_levels(rng, extent, cuts, low, largest):
    gain = 1.0
    for position, shards_of in cuts:
        draws = jax.random.uniform(jax.random.fold_in(jax.random.fold_in(rng, 6), position), (shards_of,), jnp.float32, low / len(cuts), largest / len(cuts))
        gain = gain * jnp.repeat(jnp.exp(draws), extent[position] // shards_of).reshape((-1,) + (1,) * (len(extent) - 1 - position))
    return gain


def length_profile(number_of, total, bound, slope):
    loads = [(1 << 20) // math.isqrt(rank ** slope) + 1 for rank in range(2, number_of + 1)]
    rest, holding = total - bound - (number_of - 1), [1] * (number_of - 1)
    while rest > 0:
        free = [i for i in range(number_of - 1) if holding[i] < bound]
        mass, remaining = sum([loads[i] for i in free]), rest
        for i in free:
            extra = min(bound - holding[i], max(1, remaining * loads[i] // mass), rest)
            holding[i] = holding[i] + extra
            rest = rest - extra
    return np.array([bound] + holding)


def uneven_parts(stream_key, count, total, limit, skew):
    if count == 2:
        one = jax.random.randint(stream_key, (), max(1, total - limit), min(limit, total - 1) + 1)
        return jnp.stack([one, total - one])
    sizes = jnp.asarray(length_profile(count, total, limit, skew), jnp.int32)
    couples = (count - 1) // 2
    source_of, receiver = sizes[1:1 + 2 * couples:2], sizes[2:2 + 2 * couples:2]
    room = jnp.minimum(source_of - 1, limit - receiver)
    shifted = jax.random.randint(jax.random.fold_in(stream_key, 1), (couples,), 0, 1 << 20) % (room + 1)
    sizes = sizes.at[1:1 + 2 * couples:2].set(source_of - shifted).at[2:2 + 2 * couples:2].set(receiver + shifted)
    return sizes[jax.random.permutation(jax.random.fold_in(stream_key, 2), count)]


def normal_values(stream_key, extent, scale, bound, cuts=(), kind=jnp.bfloat16):
    factor_of = block_levels(stream_key, extent, cuts, -0.22, 0.18) if cuts else 1.0
    entries = jax.random.normal(stream_key, extent, jnp.float32) * scale * factor_of
    return jnp.minimum(jnp.maximum(entries, -bound), bound).astype(kind)


def heavy_noise(own_key, shape, width, limit, cuts, heavy, held_as=jnp.bfloat16):
    entries = width * jax.random.normal(own_key, shape, jnp.float32)
    if cuts:
        entries = entries * block_levels(own_key, shape, cuts, -0.22, 0.18)
    return jnp.clip(with_spikes(entries, jax.random.fold_in(own_key, 3), *heavy), -limit, limit).astype(held_as)


def setup_inputs(seed: int = 0, part: int = 0) -> dict:
    seeds = jax.random.split(jax.random.key(seed), 13)
    part_splits = jax.random.split(jax.random.fold_in(seeds[12], part), 13)
    return {
        "train_input": heavy_noise(part_splits[0], (VIEWS, TOKENS, D), 1.0, 6.0, ((0, 2), (1, 8)), (1, 2, 8, 2.0)),
        "train_query": draw_train_query(jax.random.fold_in(jax.random.fold_in(seeds[12], part), 71), part),
        "train_keys": draw_train_keys(jax.random.fold_in(jax.random.fold_in(seeds[12], part), 71), part),
        "train_target": normal_values(part_splits[3], (VIEWS, TOKENS, Q_HEADS * HEAD_DIM), 1.0, 6.0, ((0, 2), (1, 8))),
        "train_segments": jax.vmap(lambda own: jnp.searchsorted(jnp.cumsum(uneven_parts(own, SEGMENTS, TOK_DEV, TOK_DEV // 4, 2)), jnp.arange(TOK_DEV), side="right"))(jax.random.split(part_splits[4], VIEWS * N_FSDP)).reshape((VIEWS, N_FSDP, TOK_DEV)).astype(jnp.int32),
        "value_weight": normal_values(seeds[5], (D, VALUE_WIDTH), D ** -0.5, 0.0625, ((0, 8),)),
        "adapter_down": normal_values(part_splits[6], (D, RANK), D ** -0.5, 0.0625, ((0, 8),), jnp.float32),
        "adapter_up": normal_values(part_splits[7], (RANK, VALUE_WIDTH), RANK ** -0.5, 0.75, (), jnp.float32),
        "score_input": normal_values(part_splits[8], (VIEWS, STOKENS, D), 1.0, 6.0, ((0, 2), (1, 8))),
        "score_query": draw_score_query(jax.random.fold_in(jax.random.fold_in(seeds[12], part), 71), part),
        "score_keys": draw_score_keys(jax.random.fold_in(jax.random.fold_in(seeds[12], part), 71), part),
        "score_segments": jax.vmap(lambda own: jnp.searchsorted(jnp.cumsum(uneven_parts(own, 4, SCORE_DEV, SCORE_DEV // 2, 1)), jnp.arange(SCORE_DEV), side="right"))(jax.random.split(part_splits[11], VIEWS * N_FSDP)).reshape((VIEWS, N_FSDP, SCORE_DEV)).astype(jnp.int32),
    }


adapter_scale_factor = 0.5
rate_down = 2e-05
rate_up = 0.001

def attend_row(query, keyset, value_rows, segment):
    length = query.shape[0]
    query_heads = query.reshape(length, KV_HEADS, GROUP, HEAD_DIM).astype(jnp.float32)
    key_heads = keyset.reshape(length, KV_HEADS, HEAD_DIM).astype(jnp.float32)
    logits = jnp.einsum('qgjd,kgd->gjqk', query_heads, key_heads) * HEAD_DIM ** (-0.5)
    positions = jnp.arange(length, dtype=jnp.int32)
    allowed = (positions[None, :] <= positions[:, None]) & (segment[:, None] == segment[None, :])
    logits = jnp.where(allowed, logits, -1e+30)
    peak = lax.optimization_barrier(jnp.max(logits, axis=-1, keepdims=True))
    weights = jnp.exp(logits - peak)
    probs = (weights / lax.optimization_barrier(jnp.sum(weights, axis=-1, keepdims=True))).astype(jnp.bfloat16)
    value_heads = value_rows.reshape(length, KV_HEADS, HEAD_DIM).astype(jnp.float32)
    attended = jnp.einsum('gjqk,kgd->qgjd', probs.astype(jnp.float32), value_heads)
    return (probs, attended.reshape(length, Q_HEADS * HEAD_DIM))

def values_grad(probs, d_out):
    length = d_out.shape[0]
    heads = d_out.reshape(length, KV_HEADS, GROUP, HEAD_DIM).astype(jnp.float32)
    summed = jnp.einsum('gjqk,qgjd->kgd', probs.astype(jnp.float32), heads)
    return summed.reshape(length, VALUE_WIDTH).astype(jnp.bfloat16)

def project(rows_in, value_weight, down_half, upper_weight_half):
    lower_rank_half = jnp.dot(rows_in, down_half, preferred_element_type=jnp.float32).astype(jnp.bfloat16)
    frozen_base_weight = jnp.dot(rows_in, value_weight, preferred_element_type=jnp.float32)
    value_rows = (frozen_base_weight + adapter_scale_factor * jnp.dot(lower_rank_half, upper_weight_half, preferred_element_type=jnp.float32)).astype(jnp.bfloat16)
    return (value_rows, lower_rank_half)

def reference(train_input, train_query, train_keys, train_target, train_segments, value_weight, adapter_down, adapter_up, score_input, score_query, score_keys, score_segments):
    down_half = adapter_down.astype(jnp.bfloat16)
    upper_weight_half = adapter_up.astype(jnp.bfloat16)
    train_rows = train_input.reshape(-1, D)
    value_rows, lower_rank_half = project(train_rows, value_weight, down_half, upper_weight_half)
    count_rows = VIEWS * N_FSDP

    def row_step(pieces):
        query, keyset, vals, segment, goal = pieces
        probs, attended = attend_row(query, keyset, vals, segment)
        d_out = (attended - goal.astype(jnp.float32)).astype(jnp.bfloat16)
        return values_grad(probs, d_out)
    value_output_gradient = lax.map(row_step, (train_query.reshape(count_rows, TOK_DEV, Q_HEADS * HEAD_DIM), train_keys.reshape(count_rows, TOK_DEV, VALUE_WIDTH), value_rows.reshape(count_rows, TOK_DEV, VALUE_WIDTH), train_segments.reshape(count_rows, TOK_DEV), train_target.reshape(count_rows, TOK_DEV, Q_HEADS * HEAD_DIM)))
    value_output_gradient = value_output_gradient.reshape(-1, VALUE_WIDTH)
    low_rank_gradient = (adapter_scale_factor * jnp.dot(value_output_gradient, upper_weight_half.T, preferred_element_type=jnp.float32)).astype(jnp.bfloat16)
    grad_down = jnp.dot(train_rows.T, low_rank_gradient, preferred_element_type=jnp.float32)
    up_weight_gradient = adapter_scale_factor * jnp.dot(lower_rank_half.T, value_output_gradient, preferred_element_type=jnp.float32)
    new_down = adapter_down - rate_down * grad_down
    new_up = adapter_up - rate_up * up_weight_gradient
    score_rows = score_input.reshape(-1, D)
    score_values, score_low = project(score_rows, value_weight, new_down.astype(jnp.bfloat16), new_up.astype(jnp.bfloat16))

    def score_step(pieces):
        query, keyset, vals, segment = pieces
        probs, attended = attend_row(query, keyset, vals, segment)
        return attended.astype(jnp.bfloat16)
    scored = lax.map(score_step, (score_query.reshape(count_rows, SCORE_DEV, Q_HEADS * HEAD_DIM), score_keys.reshape(count_rows, SCORE_DEV, VALUE_WIDTH), score_values.reshape(count_rows, SCORE_DEV, VALUE_WIDTH), score_segments.reshape(count_rows, SCORE_DEV)))
    return (new_down, new_up, scored.reshape(VIEWS, STOKENS, Q_HEADS * HEAD_DIM))
```

```python
import functools

import jax
import jax.numpy as jnp
from jax import lax
from jax.experimental import pallas as pl
from jax.experimental.pallas import tpu as pltpu
from jax.sharding import PartitionSpec as P

Q_HEADS = 32
KV_HEADS = 4
HEAD_DIM = 128
GROUP = 8
VALUE_WIDTH = 512
RANK = 64
UP_ROWS = 8

adapter_scale_factor = 0.5
rate_down = 2e-05
rate_up = 0.001


F32 = jnp.float32
BF16 = jnp.bfloat16
VM = pl.BlockSpec(memory_space=pltpu.VMEM)
SM = pl.BlockSpec(memory_space=pltpu.SMEM)
ANY = pl.BlockSpec(memory_space=pl.ANY)


def dot_nn(a, b):
    return lax.dot_general(a, b, (((1,), (0,)), ((), ())), preferred_element_type=F32)


def dot_nt(a, b):
    return lax.dot_general(a, b, (((1,), (1,)), ((), ())), preferred_element_type=F32)


def cost(flops, nbytes):
    return pl.CostEstimate(flops=int(flops), bytes_accessed=int(nbytes), transcendentals=0)


def call(kernel, outs, operands, specs, scratch=(), flops=1e6, name=None):
    nbytes = sum(a.size * a.dtype.itemsize for a in operands if a.size < 2**21)
    return pl.pallas_call(
        kernel,
        out_shape=[jax.ShapeDtypeStruct(s, d) for s, d in outs],
        in_specs=list(specs),
        out_specs=[VM] * len(outs),
        scratch_shapes=list(scratch),
        cost_estimate=cost(flops, nbytes),
        name=name,
    )(*operands)


def train_head_kernel(seg_row, seg_col, q_ref, k_ref, t_ref, _dep, mh_ref, ml_ref, r_ref):
    length = k_ref.shape[0]
    keys = k_ref[...]
    row = lax.broadcasted_iota(jnp.int32, (length, length), 0)
    col = lax.broadcasted_iota(jnp.int32, (length, length), 1)
    allowed = (row <= col) & (seg_col[...] == seg_row[...])
    gram = jnp.zeros((length, length), F32)
    aimed = jnp.zeros((length, HEAD_DIM), F32)
    for j in range(GROUP):
        lanes = slice(j * HEAD_DIM, (j + 1) * HEAD_DIM)
        logits = dot_nt(keys, q_ref[:, lanes]) * HEAD_DIM ** (-0.5)
        logits = jnp.where(allowed, logits, -1e30)
        peak = jnp.max(logits, axis=0, keepdims=True)
        weights = jnp.exp(logits - peak)
        probs = (weights / jnp.sum(weights, axis=0, keepdims=True)).astype(BF16)
        gram += dot_nt(probs, probs)
        aimed += dot_nn(probs, t_ref[:, lanes])
    high = gram.astype(BF16)
    mh_ref[...] = high
    ml_ref[...] = (gram - high.astype(F32)).astype(BF16)
    r_ref[...] = aimed


def train_head(g, seg_row, seg_col, query, keyset, target, dep):
    length = query.shape[0]
    width = GROUP * HEAD_DIM
    return pl.pallas_call(
        train_head_kernel,
        grid=(1,),
        out_shape=[
            jax.ShapeDtypeStruct((length, length), BF16),
            jax.ShapeDtypeStruct((length, length), BF16),
            jax.ShapeDtypeStruct((length, HEAD_DIM), F32),
        ],
        in_specs=[
            pl.BlockSpec((1, length), lambda i: (0, 0)),
            pl.BlockSpec((length, 1), lambda i: (0, 0)),
            pl.BlockSpec((length, width), lambda i: (0, g)),
            pl.BlockSpec((length, HEAD_DIM), lambda i: (0, g)),
            pl.BlockSpec((length, width), lambda i: (0, g)),
            ANY,
        ],
        out_specs=[
            pl.BlockSpec((length, length), lambda i: (0, 0)),
            pl.BlockSpec((length, length), lambda i: (0, 0)),
            pl.BlockSpec((length, HEAD_DIM), lambda i: (0, 0)),
        ],
        cost_estimate=cost(2e9, 2**21),
        name=f"train_head_{g}",
    )(seg_row, seg_col, query, keyset, target, dep)


def score_probs_kernel(seg_row, seg_col, q_ref, k_ref, _dep, p_ref):
    length = k_ref.shape[0]
    row = lax.broadcasted_iota(jnp.int32, (length, length), 0)
    col = lax.broadcasted_iota(jnp.int32, (length, length), 1)
    allowed = (col <= row) & (seg_col[...] == seg_row[...])
    for g in range(KV_HEADS):
        keys = k_ref[:, g * HEAD_DIM : (g + 1) * HEAD_DIM]
        for j in range(GROUP):
            h = g * GROUP + j
            logits = dot_nt(q_ref[:, h * HEAD_DIM : (h + 1) * HEAD_DIM], keys) * HEAD_DIM ** (-0.5)
            logits = jnp.where(allowed, logits, -1e30)
            weights = jnp.exp(logits - jnp.max(logits, axis=1, keepdims=True))
            probs = weights / jnp.sum(weights, axis=1, keepdims=True)
            p_ref[g, j * length : (j + 1) * length, :] = probs.astype(BF16)


def score_probs(seg_row, seg_col, query, keyset, dep):
    length = query.shape[0]
    return call(
        score_probs_kernel,
        [((KV_HEADS, GROUP * length, length), BF16)],
        (seg_row, seg_col, query, keyset, dep),
        (VM, VM, VM, VM, ANY),
        flops=1e9,
        name="score_probs",
    )[0]


def unpack_down(packed, half):
    parts = VALUE_WIDTH // half
    if parts == 1:
        return packed
    return jnp.concatenate([packed[:, i * half : (i + 1) * half] for i in range(parts)], axis=0)


def pack_down(block, half):
    parts = VALUE_WIDTH // half
    if parts == 1:
        return block
    rows = block.shape[0] // parts
    return jnp.concatenate([block[i * rows : (i + 1) * rows] for i in range(parts)], axis=1)


def accumulate(acc_ref, accs_ref, low_ref, x_half, xs_half, pieces):
    half = x_half.shape[1]
    for q, piece in enumerate(pieces):
        rows = half // 2
        weight = piece[:rows, :]
        acc_ref[...] += dot_nn(x_half[:, q * rows : (q + 1) * rows], weight)
        accs_ref[...] += dot_nn(xs_half[:, q * rows : (q + 1) * rows], weight)
        down = unpack_down(piece[rows:, :], half)
        lo = q * (RANK // 2)
        low_ref[lo : lo + RANK // 2, :] += dot_nt(down, x_half[...])


def own_kernel(at, w_ref, d_ref, x_hbm, xs_hbm, acc, accs, low, xb, xsb, sems):
    width = w_ref.shape[0]
    here = pl.ds(pl.multiple_of(at[0], 128), width)
    first = pltpu.make_async_copy(x_hbm.at[:, here], xb, sems.at[0])
    second = pltpu.make_async_copy(xs_hbm.at[:, here], xsb, sems.at[1])
    first.start()
    second.start()
    first.wait()
    second.wait()
    acc[...] = dot_nn(xb[...], w_ref[...])
    accs[...] = dot_nn(xsb[...], w_ref[...])
    low[...] = dot_nt(d_ref[...], xb[...])


def own_shard(at, weight, down_t, rows, score_rows):
    width = weight.shape[0]
    length, slength = rows.shape[0], score_rows.shape[0]
    return call(
        own_kernel,
        [((length, VALUE_WIDTH), F32), ((slength, VALUE_WIDTH), F32), ((RANK, length), F32)],
        (at, weight, down_t, rows, score_rows),
        (SM, VM, VM, ANY, ANY),
        scratch=(
            pltpu.VMEM((length, width), BF16),
            pltpu.VMEM((slength, width), BF16),
            pltpu.SemaphoreType.DMA((2,)),
        ),
        flops=4e8,
        name="own_shard",
    )


def x_copies(at, x_hbm, xs_hbm, xb, xsb, sems, count):
    half = xb.shape[2]
    copies = []
    for i in range(count):
        here = pl.ds(pl.multiple_of(at[i], 128), half)
        copies.append(pltpu.make_async_copy(x_hbm.at[:, here], xb.at[i], sems.at[0, i]))
        copies.append(pltpu.make_async_copy(xs_hbm.at[:, here], xsb.at[i], sems.at[1, i]))
    for c in copies:
        c.start()
    return copies


def step_kernel(count, at, acc_in, accs_in, low_in, x_hbm, xs_hbm, *refs):
    pieces, (acc, accs, low, xb, xsb, sems) = refs[: 2 * count], refs[2 * count :]
    copies = x_copies(at, x_hbm, xs_hbm, xb, xsb, sems, count)
    acc[...] = acc_in[...]
    accs[...] = accs_in[...]
    low[...] = low_in[...]
    for i in range(count):
        copies[2 * i].wait()
        copies[2 * i + 1].wait()
        accumulate(acc, accs, low, xb.at[i], xsb.at[i], pieces[2 * i : 2 * i + 2])


def step(at, sums, rows, score_rows, pieces, half, name):
    count = len(pieces) // 2
    acc, accs, low = sums
    length, slength = rows.shape[0], score_rows.shape[0]
    return call(
        functools.partial(step_kernel, count),
        [(a.shape, F32) for a in sums],
        (at, acc, accs, low, rows, score_rows, *pieces),
        (SM, VM, VM, VM, ANY, ANY) + (VM,) * len(pieces),
        scratch=(
            pltpu.VMEM((count, length, half), BF16),
            pltpu.VMEM((count, slength, half), BF16),
            pltpu.SemaphoreType.DMA((2, count)),
        ),
        flops=count * 2e8,
        name=name,
    )


def grad_kernel(count, shards, at, *refs):
    acc_in, accs_in, low_in, x_hbm, xs_hbm = refs[:5]
    pieces = refs[5 : 5 + 2 * count]
    refs = refs[5 + 2 * count :]
    grams, grams_low, aimed = refs[:4], refs[4:8], refs[8:12]
    up_ref, accs, own, send, up_grad = refs[12:17]
    acc, low, xb, xsb, x_all, sems, whole_sem = refs[17:]
    half = xb.shape[2]
    copies = x_copies(at, x_hbm, xs_hbm, xb, xsb, sems, count)
    everything = pltpu.make_async_copy(x_hbm, x_all, whole_sem)
    everything.start()
    acc[...] = acc_in[...]
    accs[...] = accs_in[...]
    low[...] = low_in[...]
    for i in range(count):
        copies[2 * i].wait()
        copies[2 * i + 1].wait()
        accumulate(acc, accs, low, xb.at[i], xsb.at[i], pieces[2 * i : 2 * i + 2])
    up_half = up_ref[...].astype(BF16)
    low_half = low[...].astype(BF16)
    low_rows = low_half.astype(F32).T.astype(BF16)
    values = (acc[...] + adapter_scale_factor * dot_nn(low_rows, up_half)).astype(BF16)
    grads = []
    for g in range(KV_HEADS):
        head = values[:, g * HEAD_DIM : (g + 1) * HEAD_DIM]
        d_head = dot_nn(grams[g][...], head) + dot_nn(grams_low[g][...], head) - aimed[g][...]
        grads.append(d_head.astype(BF16))
    d_values = jnp.concatenate(grads, axis=1)
    d_low = (adapter_scale_factor * dot_nt(up_half, d_values)).astype(BF16)
    everything.wait()
    mine, other = at[count], at[count + 1]
    for j in range(shards):
        there = pl.ds(pl.multiple_of(2 * half * j + other, 128), half)
        send[:, j * half : (j + 1) * half] = dot_nn(d_low, x_all[:, there]).astype(BF16)
    for j in range(shards):
        here = pl.ds(pl.multiple_of(2 * half * j + mine, 128), half)
        own[:, j * half : (j + 1) * half] = dot_nn(d_low, x_all[:, here])
    up_grad[...] = adapter_scale_factor * dot_nn(low_half, d_values)


def grads(at, sums, rows, score_rows, pieces, grams, grams_low, aimed, up, half, shards):
    count = len(pieces) // 2
    acc, accs, low = sums
    length, slength = rows.shape[0], score_rows.shape[0]
    return call(
        functools.partial(grad_kernel, count, shards),
        [
            (accs.shape, F32),
            ((RANK, shards * half), F32),
            ((RANK, shards * half), BF16),
            ((RANK, VALUE_WIDTH), F32),
        ],
        (at, acc, accs, low, rows, score_rows, *pieces, *grams, *grams_low, *aimed, up),
        (SM, VM, VM, VM, ANY, ANY) + (VM,) * (len(pieces) + 13),
        scratch=(
            pltpu.VMEM(acc.shape, F32),
            pltpu.VMEM(low.shape, F32),
            pltpu.VMEM((count, length, half), BF16),
            pltpu.VMEM((count, slength, half), BF16),
            pltpu.VMEM(rows.shape, BF16),
            pltpu.SemaphoreType.DMA((2, count)),
            pltpu.SemaphoreType.DMA,
        ),
        flops=1e9,
        name="grads",
    )


def split_kernel(shards, half, at, own, got, up_a, up_b, keep, keep_up, *rest):
    out, (up_sum,) = rest[: shards - 1], rest[shards - 1 :]
    up_sum[...] = up_a[...] + up_b[...]
    for k in [*range(1, shards), 0]:
        piece, row, col = at[3 * k], at[3 * k + 1], at[3 * k + 2]
        lanes = pl.ds(pl.multiple_of(piece, 128), half)
        summed = own[:, lanes] + got[:, lanes].astype(F32)
        up_piece = up_sum[pl.ds(pl.multiple_of(row, UP_ROWS), UP_ROWS), pl.ds(pl.multiple_of(col, 128), half)]
        if k == 0:
            keep[...] = summed
            keep_up[...] = up_piece
        else:
            out[k - 1][:RANK, :] = summed.astype(BF16)
            out[k - 1][RANK:, :] = up_piece.astype(BF16)


def split(at, own, got, up_a, up_b, shards, half):
    return call(
        functools.partial(split_kernel, shards, half),
        [((RANK, half), F32), ((UP_ROWS, half), F32)] + [((RANK + UP_ROWS, half), BF16)] * (shards - 1),
        (at, own, got, up_a, up_b),
        (SM, VM, VM, VM, VM),
        scratch=(pltpu.VMEM((RANK, VALUE_WIDTH), F32),),
        name="split",
    )


def update_kernel(at, keep, keep_up, down_ref, up_ref, *rest):
    got, (fresh, message) = rest[:-2], rest[-2:]
    half = keep.shape[1]
    total, total_up = keep[...], keep_up[...]
    for piece in got:
        total += piece[:RANK, :].astype(F32)
        total_up += piece[RANK:, :].astype(F32)
    new_down = down_ref[:, pl.ds(pl.multiple_of(at[0], 128), half)] - rate_down * total
    old_up = up_ref[pl.ds(pl.multiple_of(at[1], UP_ROWS), UP_ROWS), pl.ds(pl.multiple_of(at[2], 128), half)]
    new_up = old_up - rate_up * total_up
    high = new_up.astype(BF16)
    fresh[...] = new_down
    message[:RANK, :] = new_down.astype(BF16)
    message[RANK : RANK + UP_ROWS, :] = high
    message[RANK + UP_ROWS :, :] = (new_up - high.astype(F32)).astype(BF16)


def update(at, keep, keep_up, down_t, up, got):
    half = keep.shape[1]
    return call(
        update_kernel,
        [((RANK, half), F32), ((RANK + 2 * UP_ROWS, half), BF16)],
        (at, keep, keep_up, down_t, up, *got),
        (SM, VM, VM, VM, VM) + (VM,) * len(got),
        name="update",
    )


def score_low_kernel(shards, at, xs, xs_other, *rest):
    messages, (mine, other, up) = rest[:shards], rest[shards:]
    half = messages[0].shape[1]
    low_mine = jnp.zeros(mine.shape, F32)
    low_other = jnp.zeros(other.shape, F32)
    for k in range(shards):
        down = messages[k][:RANK, :]
        low_other += dot_nt(xs_other[:, pl.ds(pl.multiple_of(at[4 * k + 1], 128), half)], down)
        low_mine += dot_nt(xs[:, pl.ds(pl.multiple_of(at[4 * k], 128), half)], down)
        row, col = at[4 * k + 2], at[4 * k + 3]
        where = (pl.ds(pl.multiple_of(row, UP_ROWS), UP_ROWS), pl.ds(pl.multiple_of(col, 128), half))
        up[where] = messages[k][RANK : RANK + UP_ROWS, :].astype(F32) + messages[k][RANK + UP_ROWS :, :].astype(F32)
    mine[...] = low_mine
    other[...] = low_other


def score_low(at, score_rows, other_rows, messages):
    length = score_rows.shape[0]
    return call(
        functools.partial(score_low_kernel, len(messages)),
        [((length, RANK), F32), ((length, RANK), F32), ((RANK, VALUE_WIDTH), F32)],
        (at, score_rows, other_rows, *messages),
        (SM, VM, VM) + (VM,) * len(messages),
        name="score_low",
    )


def score_kernel(base, mine, got, up, p_ref, out):
    length = base.shape[0]
    low = (mine[...] + got[...]).astype(BF16)
    values = (base[...] + adapter_scale_factor * dot_nn(low, up[...].astype(BF16))).astype(BF16)
    for g in range(KV_HEADS):
        attended = dot_nn(p_ref[g], values[:, g * HEAD_DIM : (g + 1) * HEAD_DIM]).astype(BF16)
        for j in range(GROUP):
            h = g * GROUP + j
            out[:, h * HEAD_DIM : (h + 1) * HEAD_DIM] = attended[j * length : (j + 1) * length, :]


def score(base, mine, got, up, probs):
    length = base.shape[0]
    return call(
        score_kernel,
        [((length, Q_HEADS * HEAD_DIM), BF16)],
        (base, mine, got, up, probs),
        (VM,) * 5,
        name="score",
    )[0]


def solution(mesh):
    n_fsdp, n_view = mesh.shape["fsdp"], mesh.shape["view"]
    line = n_fsdp // 2

    def ring_device(place):
        place = place % n_fsdp
        return 2 * place if place < line else 2 * (n_fsdp - 1 - place) + 1

    forward = [(ring_device(i), ring_device(i + 1)) for i in range(n_fsdp)]
    backward = [(b, a) for a, b in forward]

    def over_view(array, bit):
        return lax.ppermute(array, "view", [(i, i ^ bit) for i in range(n_view)])

    def swap(array):
        return over_view(array, 1)

    def body(
        train_input,
        train_query,
        train_keys,
        train_target,
        train_segments,
        value_weight,
        adapter_down,
        adapter_up,
        score_input,
        score_query,
        score_keys,
        score_segments,
    ):
        width = train_input.shape[-1]
        rows = train_input.reshape(-1, width)
        score_rows = score_input.reshape(-1, width)
        query, keyset, target = (a.reshape(rows.shape[0], -1) for a in (train_query, train_keys, train_target))
        squery, skeyset = (a.reshape(score_rows.shape[0], -1) for a in (score_query, score_keys))
        shard = value_weight.shape[0]
        half = shard // 2
        me = lax.axis_index("fsdp")
        core = lax.axis_index("view") % 2
        place = jnp.where(me % 2 == 0, me // 2, n_fsdp - 1 - me // 2)

        def owner(position):
            position = position % n_fsdp
            return jnp.where(position < line, 2 * position, 2 * (n_fsdp - 1 - position) + 1)

        down_t = adapter_down.T
        down_half = down_t.astype(BF16)
        my_down = lax.dynamic_slice_in_dim(down_half, core * half, half, 1)
        my_weight = lax.dynamic_slice_in_dim(value_weight, core * half, half, 0)
        pieces = [
            jnp.concatenate(
                [
                    my_weight[q * half // 2 : (q + 1) * half // 2],
                    pack_down(my_down[q * RANK // 2 : (q + 1) * RANK // 2], half),
                ],
                axis=0,
            )
            for q in range(2)
        ]

        steps = n_fsdp // 2
        ahead, back = list(pieces), list(pieces)
        arrived = []
        for s in range(1, steps + 1):
            if s < steps:
                ahead = [lax.ppermute(a, "fsdp", forward) for a in ahead]
                back = [lax.ppermute(a, "fsdp", backward) for a in back]
                both = ahead + back
            else:
                both = [lax.ppermute(ahead[0], "fsdp", forward), lax.ppermute(back[1], "fsdp", backward)]
            arrived.append((both, [swap(a) for a in both]))

        def halves(position):
            start = owner(position) * shard
            return [start + core * half, start + (1 - core) * half]

        other_rows = score_rows.reshape(-1, n_fsdp, 2, half)
        other_rows = lax.dynamic_index_in_dim(other_rows, 1 - core, 2, False).reshape(score_rows.shape[0], -1)
        other_rows = swap(other_rows)

        seg_row = train_segments.reshape(1, -1)
        seg_col = train_segments.reshape(-1, 1)
        sseg_row = score_segments.reshape(1, -1)
        sseg_col = score_segments.reshape(-1, 1)

        sums = own_shard((me * shard)[None], value_weight, down_half, rows, score_rows)
        heads = [train_head(0, seg_row, seg_col, query, keyset, target, pieces[0])]
        order = [1, 2, 3]
        for s in range(1, steps):
            got, swapped = arrived[s - 1]
            at = jnp.stack(halves(place - s) + halves(place + s))
            sums = step(
                at, sums, rows, score_rows,
                got[:2] + swapped[:2] + got[2:] + swapped[2:], half, f"shards_{s}",
            )
            if s <= len(order):
                heads.append(train_head(order[s - 1], seg_row, seg_col, query, keyset, target, got[0]))
        probs = score_probs(sseg_row, sseg_col, squery, skeyset, arrived[0][0][2])
        got, swapped = arrived[-1]
        at = jnp.stack(halves(place + steps) + [core * half, (1 - core) * half])
        base, own, send, up_grad = grads(
            at, sums, rows, score_rows, got + swapped,
            [h[0] for h in heads], [h[1] for h in heads], [h[2] for h in heads],
            adapter_up, half, n_fsdp,
        )

        got, up_got = swap(send), swap(up_grad)
        bit = 2
        while bit < n_view:
            own = (own + got.astype(F32)).astype(BF16)
            got = over_view(own, bit)
            own = own.astype(F32)
            up_grad = up_grad + up_got
            up_got = over_view(up_grad, bit)
            bit *= 2

        columns = VALUE_WIDTH // half

        def up_place(device):
            return [(device // columns) * UP_ROWS, (device % columns) * half]

        at = jnp.stack([v for k in range(n_fsdp) for v in [(me ^ k) * half, *up_place(me ^ k)]])
        keep, keep_up, *out = split(at, own, got, up_grad, up_got, n_fsdp, half)

        def exchange(array, k):
            return lax.ppermute(array, "fsdp", [(i, i ^ k) for i in range(n_fsdp)])

        got = [exchange(a, k + 1) for k, a in enumerate(out)]
        at = jnp.stack([core * half, *up_place(me)])
        fresh, message = update(at, keep, keep_up, down_t, adapter_up, got)
        messages = [message] + [exchange(message, k) for k in range(1, n_fsdp)]
        fresh_other = swap(fresh)

        at = jnp.stack(
            [v for k in range(n_fsdp) for v in [(me ^ k) * shard + core * half, (me ^ k) * half, *up_place(me ^ k)]]
        )
        mine, other, new_up = score_low(at, score_rows, other_rows, messages)
        scored = score(base, mine, swap(other), new_up, probs)
        new_down = jnp.where(
            core == 0,
            jnp.concatenate([fresh, fresh_other], axis=1),
            jnp.concatenate([fresh_other, fresh], axis=1),
        ).T
        return (new_down, new_up, scored.reshape(score_query.shape))

    in_specs = (
        P(("task", "view"), "fsdp", None),
        P(("task", "view"), "fsdp", None),
        P(("task", "view"), "fsdp", None),
        P(("task", "view"), "fsdp", None),
        P(("task", "view"), "fsdp", None),
        P("fsdp", None),
        P(("task", "fsdp"), None),
        P("task", None),
        P(("task", "view"), "fsdp", None),
        P(("task", "view"), "fsdp", None),
        P(("task", "view"), "fsdp", None),
        P(("task", "view"), "fsdp", None),
    )
    out_specs = (P(("task", "fsdp"), None), P("task", None), P(("task", "view"), "fsdp", None))
    return jax.shard_map(body, mesh=mesh, in_specs=in_specs, out_specs=out_specs, check_vma=False)
```

```python
import functools

import jax
import jax.numpy as jnp
from jax import lax
from jax.experimental import pallas as pl
from jax.experimental.pallas import tpu as pltpu
from jax.sharding import PartitionSpec as P

Q_HEADS = 32
KV_HEADS = 4
HEAD_DIM = 128
GROUP = 8
VALUE_WIDTH = 512
RANK = 64
UP_ROWS = 8

adapter_scale_factor = 0.5
rate_down = 2e-05
rate_up = 0.001


F32 = jnp.float32
BF16 = jnp.bfloat16
VM = pl.BlockSpec(memory_space=pltpu.VMEM)
SM = pl.BlockSpec(memory_space=pltpu.SMEM)
ANY = pl.BlockSpec(memory_space=pl.ANY)
VMEM_GRANT = 16 * 2**20


def dot_nn(a, b):
    return lax.dot_general(a, b, (((1,), (0,)), ((), ())), preferred_element_type=F32)


def dot_nt(a, b):
    return lax.dot_general(a, b, (((1,), (1,)), ((), ())), preferred_element_type=F32)


def cost(flops, nbytes):
    return pl.CostEstimate(flops=int(flops), bytes_accessed=int(nbytes), transcendentals=0)


def near(array):
    return pltpu.with_memory_space_constraint(array, pltpu.VMEM)


def call(kernel, outs, scalars, operands, scratch=(), flops=1e6, name=None, final=(), deps=()):
    n, d = len(operands), len(deps)

    def whole(scalar_ref, *refs):
        kernel(scalar_ref, refs[:n], refs[n + d : n + d + len(outs)], refs[n + d + len(outs) :])

    return pl.pallas_call(
        whole,
        out_shape=[jax.ShapeDtypeStruct(*o) if i in final else pltpu.VMEM(*o) for i, o in enumerate(outs)],
        in_specs=[SM] + [VM] * n + [ANY] * d,
        out_specs=[VM] * len(outs),
        scratch_shapes=list(scratch),
        cost_estimate=cost(flops, 2**20),
        compiler_params=pltpu.CompilerParams(vmem_limit_bytes=VMEM_GRANT),
        name=name,
    )(scalars, *[near(a) for a in operands], *deps)


def lanes_at(start, size):
    return pl.ds(pl.multiple_of(start, 128), size)


def train_head_kernel(g, s, refs, outs, scratch):
    seg_row, seg_col, q_ref, k_ref, t_ref = refs
    high_out, rest_out, aimed_out = outs
    length = k_ref.shape[0]
    keys = k_ref[:, g * HEAD_DIM : (g + 1) * HEAD_DIM]
    row = lax.broadcasted_iota(jnp.int32, (length, length), 0)
    col = lax.broadcasted_iota(jnp.int32, (length, length), 1)
    allowed = (row <= col) & (seg_col[...] == seg_row[...])
    lanes = [slice(h * HEAD_DIM, (h + 1) * HEAD_DIM) for h in range(g * GROUP, (g + 1) * GROUP)]
    every = []
    for j in range(GROUP):
        logits = dot_nt(keys, q_ref[:, lanes[j]]) * HEAD_DIM ** (-0.5)
        logits = jnp.where(allowed, logits, -1e30)
        peak = jnp.max(logits, axis=0, keepdims=True)
        weights = jnp.exp(logits - peak)
        every.append((weights / jnp.sum(weights, axis=0, keepdims=True)).astype(BF16))
    gram = sum(dot_nt(probs, probs) for probs in every)
    high = gram.astype(BF16)
    high_out[...] = high
    rest_out[...] = (gram - high.astype(F32)).astype(BF16)
    aimed_out[...] = sum(dot_nn(probs, t_ref[:, lanes[j]]) for j, probs in enumerate(every))


def train_head(s, g, seg_row, seg_col, query, keyset, target, deps):
    length = query.shape[0]
    return call(
        functools.partial(train_head_kernel, g),
        [((length, length), BF16), ((length, length), BF16), ((length, HEAD_DIM), F32)],
        s, [seg_row, seg_col, query, keyset, target], flops=2e9, name=f"train_head_{g}", deps=deps,
    )


def score_probs_kernel(s, refs, outs, scratch):
    seg_row, seg_col, q_ref, k_ref = refs
    (p_ref,) = outs
    length = k_ref.shape[0]
    row = lax.broadcasted_iota(jnp.int32, (length, length), 0)
    col = lax.broadcasted_iota(jnp.int32, (length, length), 1)
    allowed = (col <= row) & (seg_col[...] == seg_row[...])
    for g in range(KV_HEADS):
        keys = k_ref[:, g * HEAD_DIM : (g + 1) * HEAD_DIM]
        for j in range(GROUP):
            h = g * GROUP + j
            logits = dot_nt(q_ref[:, h * HEAD_DIM : (h + 1) * HEAD_DIM], keys) * HEAD_DIM ** (-0.5)
            logits = jnp.where(allowed, logits, -1e30)
            weights = jnp.exp(logits - jnp.max(logits, axis=1, keepdims=True))
            probs = weights / jnp.sum(weights, axis=1, keepdims=True)
            p_ref[g, j * length : (j + 1) * length, :] = probs.astype(BF16)


def score_probs(s, seg_row, seg_col, query, keyset, deps):
    length = query.shape[0]
    return call(
        score_probs_kernel, [((KV_HEADS, GROUP * length, length), BF16)],
        s, [seg_row, seg_col, query, keyset], flops=1e9, name="score_probs", deps=deps,
    )[0]


def unpack_down(packed, half):
    parts = VALUE_WIDTH // half
    if parts == 1:
        return packed
    return jnp.concatenate([packed[:, i * half : (i + 1) * half] for i in range(parts)], axis=0)


def pack_down(block, half):
    parts = VALUE_WIDTH // half
    if parts == 1:
        return block
    rows = block.shape[0] // parts
    return jnp.concatenate([block[i * rows : (i + 1) * rows] for i in range(parts)], axis=1)


def low_of(pieces, half):
    return jnp.concatenate([unpack_down(p[half // 2 :, :], half) for p in pieces], axis=0)


def features_of(scalars, position, n, shard, half, core):
    position = lax.rem(position, n)
    owner = jnp.where(position < n // 2, 2 * position, 2 * (n - 1 - position) + 1)
    return owner * shard + core * half


def project_kernel(n, offsets, half, s, refs, outs, scratch):
    x, xo, xs, xso = refs[:4]
    refs = refs[4:]
    (xb,) = scratch
    t, u = x.shape[0], xs.shape[0]
    rows = half // 2
    total = low = None
    for i, offset in enumerate(offsets):
        here = lanes_at(features_of(s, s[2] + offset, n, 2 * half, half, s[1]), half)
        for at, a in ((0, x), (t, xo), (2 * t, xs), (2 * t + u, xso)):
            xb[i, at : at + a.shape[0], :] = a[:, here]
        pieces = [refs[2 * i][...], refs[2 * i + 1][...]]
        weight = jnp.concatenate([p[:rows, :] for p in pieces], axis=0)
        part = dot_nn(xb[i], weight)
        total = part if total is None else total + part
        part = dot_nt(low_of(pieces, half), xb[i, : 2 * t, :])
        low = part if low is None else low + part
    before = refs[2 * len(offsets) :]
    if before:
        total = total + before[0][...]
        low = low + before[1][...]
    if outs[0].shape[0] == total.shape[0]:
        outs[0][...] = total
        outs[1][...] = low
        return
    for i, out in enumerate(outs):
        out[:t, :] = total[i * t : (i + 1) * t, :]
        out[t : t + u, :] = total[2 * t + i * u : 2 * t + (i + 1) * u, :]
        part = low[:, i * t : (i + 1) * t]
        out[t + u :, :t] = part[: RANK // 2, :]
        out[t + u :, t : 2 * t] = part[RANK // 2 :, :]


def project(s, n, offsets, half, pieces, before, raw, final, name):
    t, u = raw[0].shape[0], raw[2].shape[0]
    if final:
        outs = [((t + u + RANK // 2, VALUE_WIDTH), F32)] * 2
    else:
        outs = [((2 * t + 2 * u, VALUE_WIDTH), F32), ((RANK, 2 * t), F32)]
    return call(
        functools.partial(project_kernel, n, offsets, half),
        outs, s, [*raw, *pieces, *before],
        scratch=[pltpu.VMEM((len(offsets), 2 * t + 2 * u, half), BF16)],
        flops=len(offsets) * 3.4e8, name=name,
    )


def grad_kernel(n, offset, half, s, refs, outs, scratch):
    x, xs = refs[:2]
    pieces, (mine, got, up_ref), heads = refs[2:6], refs[6:9], refs[9:]
    base, d_low_out, up_grad = outs
    t, u = x.shape[0], xs.shape[0]
    rows = half // 2
    total = mine[:t, :] + got[:t, :]
    base_total = mine[t : t + u, :] + got[t : t + u, :]
    packed = mine[t + u :, :] + got[t + u :, :]
    low = jnp.concatenate([packed[:, :t], packed[:, t : 2 * t]], axis=0)
    for i in range(2):
        core = s[1] if i == 0 else 1 - s[1]
        here = lanes_at(features_of(s, s[2] + offset, n, 2 * half, half, core), half)
        pair = [pieces[2 * i][...], pieces[2 * i + 1][...]]
        weight = jnp.concatenate([p[:rows, :] for p in pair], axis=0)
        total = total + dot_nn(x[:, here], weight)
        base_total = base_total + dot_nn(xs[:, here], weight)
        low = low + dot_nt(low_of(pair, half), x[:, here])
    base[...] = base_total
    low = low.astype(BF16)
    up_half = up_ref[...].astype(BF16)
    low_rows = low.astype(F32).T.astype(BF16)
    values = (total + adapter_scale_factor * dot_nn(low_rows, up_half)).astype(BF16)
    grads = []
    for g in range(KV_HEADS):
        head = values[:, g * HEAD_DIM : (g + 1) * HEAD_DIM]
        high, rest, aimed = heads[3 * g : 3 * g + 3]
        d_head = dot_nn(high[...], head) + dot_nn(rest[...], head) - aimed[...]
        grads.append(d_head.astype(BF16))
    d_values = jnp.concatenate(grads, axis=1)
    d_low_out[...] = (adapter_scale_factor * dot_nt(up_half, d_values)).astype(BF16)
    up_grad[...] = adapter_scale_factor * dot_nn(low, d_values)


def value_grads(s, n, offset, half, pieces, mine, got, up, heads, raw):
    t, u = raw[0].shape[0], raw[1].shape[0]
    return call(
        functools.partial(grad_kernel, n, offset, half),
        [((u, VALUE_WIDTH), F32), ((RANK, t), BF16), ((RANK, VALUE_WIDTH), F32)],
        s, [*raw, *pieces, mine, got, up, *[a for h in heads for a in h]],
        flops=1e9, name="value_grads",
    )


def up_place(device, half):
    columns = VALUE_WIDTH // half
    row = pl.multiple_of(lax.div(device, columns) * UP_ROWS, UP_ROWS)
    col = lax.rem(device, columns) * half
    return pl.ds(row, UP_ROWS), lanes_at(col, half)


def down_kernel(n, half, s, refs, outs, scratch):
    x, xo, d_low, d_low_got, up_grad, up_got = refs
    (up_sum,) = scratch
    keep, keep_up, *out = outs
    up_sum[...] = up_grad[...] + up_got[...]
    for k in [*range(n - 1, 0, -1), 0]:
        here = lanes_at((s[0] ^ k) * 2 * half + s[1] * half, half)
        part = dot_nn(d_low[...], x[:, here]) + dot_nn(d_low_got[...], xo[:, here])
        up_piece = up_sum[up_place(s[0] ^ k, half)]
        if k == 0:
            keep[...] = part
            keep_up[...] = up_piece
        else:
            out[k - 1][:RANK, :] = part.astype(BF16)
            out[k - 1][RANK:, :] = up_piece.astype(BF16)


def down_pieces(s, n, half, d_low, d_low_got, up_grad, up_got, raw):
    return call(
        functools.partial(down_kernel, n, half),
        [((RANK, half), F32), ((UP_ROWS, half), F32)] + [((RANK + UP_ROWS, half), BF16)] * (n - 1),
        s, [*raw, d_low, d_low_got, up_grad, up_got],
        scratch=[pltpu.VMEM((RANK, VALUE_WIDTH), F32)], flops=1e9, name="down_pieces",
    )


def update_kernel(s, refs, outs, scratch):
    keep, keep_up, down_ref, up_ref, *got = refs
    fresh, message = outs
    half = fresh.shape[1]
    old_down = down_ref[:, lanes_at(s[1] * half, half)]
    old_up = up_ref[up_place(s[0], half)]
    total, total_up = keep[...], keep_up[...]
    for piece in got:
        total += piece[:RANK, :].astype(F32)
        total_up += piece[RANK:, :].astype(F32)
    new_down = old_down - rate_down * total
    new_up = old_up - rate_up * total_up
    high = new_up.astype(BF16)
    fresh[...] = new_down
    message[:RANK, :] = new_down.astype(BF16)
    message[RANK : RANK + UP_ROWS, :] = high
    message[RANK + UP_ROWS :, :] = (new_up - high.astype(F32)).astype(BF16)


def update(s, keep, keep_up, down_t, up, got):
    half = keep.shape[1]
    return call(
        update_kernel,
        [((RANK, half), F32), ((RANK + 2 * UP_ROWS, half), BF16)],
        s, [keep, keep_up, down_t, up, *got], name="update",
    )


def score_low_kernel(n, half, s, refs, outs, scratch):
    xs, xso, *messages = refs
    mine, other, up = outs
    low_mine = low_other = None
    for k in range(n):
        here = lanes_at((s[0] ^ k) * 2 * half + s[1] * half, half)
        message = messages[k]
        part = dot_nt(xs[:, here], message[:RANK, :])
        low_mine = part if low_mine is None else low_mine + part
        part = dot_nt(xso[:, here], message[:RANK, :])
        low_other = part if low_other is None else low_other + part
        high = message[RANK : RANK + UP_ROWS, :].astype(F32)
        up[up_place(s[0] ^ k, half)] = high + message[RANK + UP_ROWS :, :].astype(F32)
    mine[...] = low_mine
    other[...] = low_other


def score_low(s, half, messages, raw):
    n, u = len(messages), raw[0].shape[0]
    return call(
        functools.partial(score_low_kernel, n, half),
        [((u, RANK), F32), ((u, RANK), F32), ((RANK, VALUE_WIDTH), F32)],
        s, [*raw, *messages], flops=2e8, name="score_low",
    )


def score_kernel(s, refs, outs, scratch):
    base, mine, got, up, probs, fresh, fresh_got = refs
    out, new_down, new_up = outs
    half = new_down.shape[1] // 2
    low = (mine[...] + got[...]).astype(BF16)
    u = low.shape[0]
    values = base[...] + adapter_scale_factor * dot_nn(low, up[...].astype(BF16))
    values = values.astype(BF16)
    for g in range(KV_HEADS):
        attended = dot_nn(probs[g], values[:, g * HEAD_DIM : (g + 1) * HEAD_DIM]).astype(BF16)
        for j in range(GROUP):
            h = g * GROUP + j
            out[:, h * HEAD_DIM : (h + 1) * HEAD_DIM] = attended[j * u : (j + 1) * u, :]
    new_down[:, lanes_at(s[1] * half, half)] = fresh[...]
    new_down[:, lanes_at((1 - s[1]) * half, half)] = fresh_got[...]
    new_up[...] = up[...]


def score(s, base, mine, got, up, probs, fresh, fresh_got):
    u, half = base.shape[0], fresh.shape[1]
    return call(
        score_kernel,
        [((u, Q_HEADS * HEAD_DIM), BF16), ((RANK, 2 * half), F32), (up.shape, F32)],
        s, [base, mine, got, up, probs, fresh, fresh_got], flops=2e8, name="score", final=(0, 1, 2),
    )


def solution(mesh):
    n_fsdp, n_view = mesh.shape["fsdp"], mesh.shape["view"]
    line = n_fsdp // 2

    def ring_device(place):
        place = place % n_fsdp
        return 2 * place if place < line else 2 * (n_fsdp - 1 - place) + 1

    forward = [(ring_device(i), ring_device(i + 1)) for i in range(n_fsdp)]
    backward = [(b, a) for a, b in forward]

    def over_view(array, bit):
        return lax.ppermute(array, "view", [(i, i ^ bit) for i in range(n_view)])

    def swap(array):
        return over_view(array, 1)

    def exchange(array, k):
        return lax.ppermute(array, "fsdp", [(i, i ^ k) for i in range(n_fsdp)])

    def body(
        train_input,
        train_query,
        train_keys,
        train_target,
        train_segments,
        value_weight,
        adapter_down,
        adapter_up,
        score_input,
        score_query,
        score_keys,
        score_segments,
    ):
        width = train_input.shape[-1]
        x = train_input.reshape(-1, width)
        xs = score_input.reshape(-1, width)
        query, keyset, target = (a.reshape(x.shape[0], -1) for a in (train_query, train_keys, train_target))
        squery, skeyset = (a.reshape(xs.shape[0], -1) for a in (score_query, score_keys))
        shard = value_weight.shape[0]
        half = shard // 2
        me = lax.axis_index("fsdp")
        core = lax.axis_index("view") % 2
        place = jnp.where(me % 2 == 0, me // 2, n_fsdp - 1 - me // 2)
        s = jnp.stack([me, core, place]).astype(jnp.int32)

        down_t = adapter_down.T
        down_half = down_t.astype(BF16)
        my_down = lax.dynamic_slice_in_dim(down_half, core * half, half, 1)
        my_weight = lax.dynamic_slice_in_dim(value_weight, core * half, half, 0)
        pieces = [
            jnp.concatenate(
                [
                    my_weight[q * half // 2 : (q + 1) * half // 2],
                    pack_down(my_down[q * RANK // 2 : (q + 1) * RANK // 2], half),
                ],
                axis=0,
            )
            for q in range(2)
        ]

        seg_row, seg_col = train_segments.reshape(1, -1), train_segments.reshape(-1, 1)
        sseg_row, sseg_col = score_segments.reshape(1, -1), score_segments.reshape(-1, 1)
        near_query, near_keys, near_target = near(query), near(keyset), near(target)

        def head(g, deps):
            return train_head(s, g, seg_row, seg_col, near_query, near_keys, near_target, deps)

        def after(arrays, work):
            return lax.optimization_barrier((arrays, work))

        def onward(ahead, back):
            return (
                [lax.ppermute(a, "fsdp", forward) for a in ahead],
                [lax.ppermute(a, "fsdp", backward) for a in back],
            )

        xo, xso = swap(x), swap(xs)
        raw = tuple(near(a) for a in (x, xo, xs, xso))
        steps = n_fsdp // 2
        arrived, offsets = list(pieces), [0]
        ahead, back = list(pieces), list(pieces)
        heads = []
        for k in range(1, steps):
            ahead, back = onward(ahead, back)
            if k == 1:
                work = [head(0, ()), score_probs(s, sseg_row, sseg_col, squery, skeyset, ())]
                ahead[0], (first, probs) = after(ahead[0], work)
                heads.append(first)
            elif k == 2:
                work = [head(1, (arrived[2],)), head(2, (arrived[2],))]
                ahead[0], work = after(ahead[0], work)
                heads += work
            elif k == 3:
                partial = project(s, n_fsdp, offsets, half, arrived, (), raw, False, "project_first")
                cut = len(offsets)
                ahead[0], partial = after(ahead[0], partial)
            arrived += [*ahead, *back]
            offsets += [n_fsdp - k, k]
        last = [lax.ppermute(ahead[0], "fsdp", forward), lax.ppermute(back[1], "fsdp", backward)]
        sums, sums_out = project(
            s, n_fsdp, offsets[cut:], half, arrived[2 * cut :], partial, raw, True, "project_second"
        )
        heads.append(head(3, (arrived[-1],)))
        sums_got = swap(sums_out)
        last[0], (sums, heads[3]) = after(last[0], (sums, heads[3]))
        last += [swap(a) for a in last]
        base, d_low, up_grad = value_grads(
            s, n_fsdp, steps, half, last, sums, sums_got, adapter_up, heads, (raw[0], raw[2])
        )

        keep, keep_up, *out = down_pieces(
            s, n_fsdp, half, d_low, swap(d_low), up_grad, swap(up_grad), raw[:2]
        )
        bit = 2
        while bit < n_view:
            keep, keep_up = (a + over_view(a, bit) for a in (keep, keep_up))
            out = [(a.astype(F32) + over_view(a, bit).astype(F32)).astype(BF16) for a in out]
            bit *= 2

        got = [exchange(a, k + 1) for k, a in enumerate(out)]
        fresh, message = update(s, keep, keep_up, down_t, adapter_up, got)
        messages = [message] + [exchange(message, k) for k in range(2, n_fsdp, 2)]
        messages = [m for a in messages for m in (a, exchange(a, 1))]
        mine, other, new_up = score_low(s, half, messages, raw[2:])
        scored, new_down, new_up = score(s, base, mine, swap(other), new_up, probs, fresh, swap(fresh))
        return (new_down.T, new_up, scored.reshape(score_query.shape))

    in_specs = (
        P(("task", "view"), "fsdp", None),
        P(("task", "view"), "fsdp", None),
        P(("task", "view"), "fsdp", None),
        P(("task", "view"), "fsdp", None),
        P(("task", "view"), "fsdp", None),
        P("fsdp", None),
        P(("task", "fsdp"), None),
        P("task", None),
        P(("task", "view"), "fsdp", None),
        P(("task", "view"), "fsdp", None),
        P(("task", "view"), "fsdp", None),
        P(("task", "view"), "fsdp", None),
    )
    out_specs = (P(("task", "fsdp"), None), P("task", None), P(("task", "view"), "fsdp", None))
    return jax.shard_map(body, mesh=mesh, in_specs=in_specs, out_specs=out_specs, check_vma=False)
```

```python
import functools

import jax
import jax.numpy as jnp
from jax import lax
from jax.experimental import pallas as pl
from jax.experimental.pallas import tpu as pltpu
from jax.sharding import PartitionSpec as P


Q_HEADS = 32
KV_HEADS = 4
HEAD_DIM = 128
GROUP = 8
VALUE_WIDTH = 512
RANK = 64
UP_ROWS = 8

adapter_scale_factor = 0.5
rate_down = 2e-05
rate_up = 0.001


F32 = jnp.float32
BF16 = jnp.bfloat16
VM = pl.BlockSpec(memory_space=pltpu.VMEM)
SM = pl.BlockSpec(memory_space=pltpu.SMEM)
ANY = pl.BlockSpec(memory_space=pl.ANY)
VMEM_GRANT = 16 * 2**20


def dot_nn(a, b):
    return lax.dot_general(a, b, (((1,), (0,)), ((), ())), preferred_element_type=F32)


def dot_nt(a, b):
    return lax.dot_general(a, b, (((1,), (1,)), ((), ())), preferred_element_type=F32)


def cost(flops, nbytes):
    return pl.CostEstimate(flops=int(flops), bytes_accessed=int(nbytes), transcendentals=0)


def near(array):
    return pltpu.with_memory_space_constraint(array, pltpu.VMEM)


def call(kernel, outs, scalars, operands, scratch=(), flops=1e6, final=(), deps=()):
    n, d = len(operands), len(deps)

    def whole(scalar_ref, *refs):
        kernel(scalar_ref, refs[:n], refs[n + d : n + d + len(outs)], refs[n + d + len(outs) :])

    return pl.pallas_call(
        whole,
        out_shape=[jax.ShapeDtypeStruct(*o) if i in final else pltpu.VMEM(*o) for i, o in enumerate(outs)],
        in_specs=[SM] + [VM] * n + [ANY] * d,
        out_specs=[VM] * len(outs),
        scratch_shapes=list(scratch),
        cost_estimate=cost(flops, 2**20),
        compiler_params=pltpu.CompilerParams(vmem_limit_bytes=VMEM_GRANT),
    )(scalars, *[near(a) for a in operands], *deps)


def lanes_at(start, size):
    return pl.ds(pl.multiple_of(start, 128), size)


def train_head_kernel(g, s, refs, outs, scratch):
    seg_row, seg_col, q_ref, k_ref, t_ref = refs
    high_out, rest_out, aimed_out = outs
    length = k_ref.shape[0]
    keys = k_ref[:, g * HEAD_DIM : (g + 1) * HEAD_DIM]
    row = lax.broadcasted_iota(jnp.int32, (length, length), 0)
    col = lax.broadcasted_iota(jnp.int32, (length, length), 1)
    allowed = (row <= col) & (seg_col[...] == seg_row[...])
    lanes = [slice(h * HEAD_DIM, (h + 1) * HEAD_DIM) for h in range(g * GROUP, (g + 1) * GROUP)]
    every = []
    for j in range(GROUP):
        logits = dot_nt(keys, q_ref[:, lanes[j]]) * HEAD_DIM ** (-0.5)
        logits = jnp.where(allowed, logits, -1e30)
        peak = jnp.max(logits, axis=0, keepdims=True)
        weights = jnp.exp(logits - peak)
        every.append((weights / jnp.sum(weights, axis=0, keepdims=True)).astype(BF16))
    gram = sum(dot_nt(probs, probs) for probs in every)
    high = gram.astype(BF16)
    high_out[...] = high
    rest_out[...] = (gram - high.astype(F32)).astype(BF16)
    aimed_out[...] = sum(dot_nn(probs, t_ref[:, lanes[j]]) for j, probs in enumerate(every))


def train_head(s, g, seg_row, seg_col, query, keyset, target, deps):
    length = query.shape[0]
    return call(
        functools.partial(train_head_kernel, g),
        [((length, length), BF16), ((length, length), BF16), ((length, HEAD_DIM), F32)],
        s, [seg_row, seg_col, query, keyset, target], flops=2e9, deps=deps,
    )


def score_probs_kernel(s, refs, outs, scratch):
    seg_row, seg_col, q_ref, k_ref = refs
    (p_ref,) = outs
    length = k_ref.shape[0]
    row = lax.broadcasted_iota(jnp.int32, (length, length), 0)
    col = lax.broadcasted_iota(jnp.int32, (length, length), 1)
    allowed = (col <= row) & (seg_col[...] == seg_row[...])
    for g in range(KV_HEADS):
        keys = k_ref[:, g * HEAD_DIM : (g + 1) * HEAD_DIM]
        for j in range(GROUP):
            h = g * GROUP + j
            logits = dot_nt(q_ref[:, h * HEAD_DIM : (h + 1) * HEAD_DIM], keys) * HEAD_DIM ** (-0.5)
            logits = jnp.where(allowed, logits, -1e30)
            weights = jnp.exp(logits - jnp.max(logits, axis=1, keepdims=True))
            probs = weights / jnp.sum(weights, axis=1, keepdims=True)
            p_ref[g, j * length : (j + 1) * length, :] = probs.astype(BF16)


def score_probs(s, seg_row, seg_col, query, keyset, deps):
    length = query.shape[0]
    return call(
        score_probs_kernel, [((KV_HEADS, GROUP * length, length), BF16)],
        s, [seg_row, seg_col, query, keyset], flops=1e9, deps=deps,
    )[0]


def unpack_down(packed, half):
    parts = VALUE_WIDTH // half
    if parts == 1:
        return packed
    return jnp.concatenate([packed[:, i * half : (i + 1) * half] for i in range(parts)], axis=0)


def pack_down(block, half):
    parts = VALUE_WIDTH // half
    if parts == 1:
        return block
    rows = block.shape[0] // parts
    return jnp.concatenate([block[i * rows : (i + 1) * rows] for i in range(parts)], axis=1)


def low_of(pieces, half):
    return jnp.concatenate([unpack_down(p[half // 2 :, :], half) for p in pieces], axis=0)


def features_of(position, n, shard, half, core):
    position = lax.rem(position, n)
    owner = jnp.where(position < n // 2, 2 * position, 2 * (n - 1 - position) + 1)
    return owner * shard + core * half


def project_kernel(n, offsets, half, s, refs, outs, scratch):
    x, xo, xs, xso = refs[:4]
    refs = refs[4:]
    (xb,) = scratch
    t, u = x.shape[0], xs.shape[0]
    rows = half // 2
    total = low = None
    for i, offset in enumerate(offsets):
        here = lanes_at(features_of(s[2] + offset, n, 2 * half, half, s[1]), half)
        for at, a in ((0, x), (t, xo), (2 * t, xs), (2 * t + u, xso)):
            xb[i, at : at + a.shape[0], :] = a[:, here]
        pieces = [refs[2 * i][...], refs[2 * i + 1][...]]
        weight = jnp.concatenate([p[:rows, :] for p in pieces], axis=0)
        part = dot_nn(xb[i], weight)
        total = part if total is None else total + part
        part = dot_nt(low_of(pieces, half), xb[i, : 2 * t, :])
        low = part if low is None else low + part
    before = refs[2 * len(offsets) :]
    if before:
        total = total + before[0][...]
        low = low + before[1][...]
    if outs[0].shape[0] == total.shape[0]:
        outs[0][...] = total
        outs[1][...] = low
        return
    for i, out in enumerate(outs):
        out[:t, :] = total[i * t : (i + 1) * t, :]
        out[t : t + u, :] = total[2 * t + i * u : 2 * t + (i + 1) * u, :]
        part = low[:, i * t : (i + 1) * t]
        out[t + u :, :t] = part[: RANK // 2, :]
        out[t + u :, t : 2 * t] = part[RANK // 2 :, :]


def project(s, n, offsets, half, pieces, before, raw, final):
    t, u = raw[0].shape[0], raw[2].shape[0]
    if final:
        outs = [((t + u + RANK // 2, VALUE_WIDTH), F32)] * 2
    else:
        outs = [((2 * t + 2 * u, VALUE_WIDTH), F32), ((RANK, 2 * t), F32)]
    return call(
        functools.partial(project_kernel, n, offsets, half),
        outs, s, [*raw, *pieces, *before],
        scratch=[pltpu.VMEM((len(offsets), 2 * t + 2 * u, half), BF16)],
        flops=len(offsets) * 3.4e8,
    )


def grad_kernel(n, offset, half, s, refs, outs, scratch):
    x, xs = refs[:2]
    pieces, (mine, got, up_ref), heads = refs[2:6], refs[6:9], refs[9:]
    base, d_low_out, up_grad = outs
    t, u = x.shape[0], xs.shape[0]
    rows = half // 2
    total = mine[:t, :] + got[:t, :]
    base_total = mine[t : t + u, :] + got[t : t + u, :]
    packed = mine[t + u :, :] + got[t + u :, :]
    low = jnp.concatenate([packed[:, :t], packed[:, t : 2 * t]], axis=0)
    for i in range(2):
        core = s[1] if i == 0 else 1 - s[1]
        here = lanes_at(features_of(s[2] + offset, n, 2 * half, half, core), half)
        pair = [pieces[2 * i][...], pieces[2 * i + 1][...]]
        weight = jnp.concatenate([p[:rows, :] for p in pair], axis=0)
        total = total + dot_nn(x[:, here], weight)
        base_total = base_total + dot_nn(xs[:, here], weight)
        low = low + dot_nt(low_of(pair, half), x[:, here])
    base[...] = base_total
    low = low.astype(BF16)
    up_half = up_ref[...].astype(BF16)
    low_rows = low.astype(F32).T.astype(BF16)
    values = (total + adapter_scale_factor * dot_nn(low_rows, up_half)).astype(BF16)
    grads = []
    for g in range(KV_HEADS):
        head = values[:, g * HEAD_DIM : (g + 1) * HEAD_DIM]
        high, rest, aimed = heads[3 * g : 3 * g + 3]
        d_head = dot_nn(high[...], head) + dot_nn(rest[...], head) - aimed[...]
        grads.append(d_head.astype(BF16))
    d_values = jnp.concatenate(grads, axis=1)
    d_low_out[...] = (adapter_scale_factor * dot_nt(up_half, d_values)).astype(BF16)
    up_grad[...] = adapter_scale_factor * dot_nn(low, d_values)


def value_grads(s, n, offset, half, pieces, mine, got, up, heads, raw):
    t, u = raw[0].shape[0], raw[1].shape[0]
    return call(
        functools.partial(grad_kernel, n, offset, half),
        [((u, VALUE_WIDTH), F32), ((RANK, t), BF16), ((RANK, VALUE_WIDTH), F32)],
        s, [*raw, *pieces, mine, got, up, *[a for h in heads for a in h]],
        flops=1e9,
    )


def up_place(device, half):
    columns = VALUE_WIDTH // half
    row = pl.multiple_of(lax.div(device, columns) * UP_ROWS, UP_ROWS)
    col = lax.rem(device, columns) * half
    return pl.ds(row, UP_ROWS), lanes_at(col, half)


def down_kernel(n, half, s, refs, outs, scratch):
    x, xo, d_low, d_low_got, up_grad, up_got = refs
    (up_sum,) = scratch
    keep, keep_up, *out = outs
    up_sum[...] = up_grad[...] + up_got[...]
    for k in [*range(n - 1, 0, -1), 0]:
        here = lanes_at((s[0] ^ k) * 2 * half + s[1] * half, half)
        part = dot_nn(d_low[...], x[:, here]) + dot_nn(d_low_got[...], xo[:, here])
        up_piece = up_sum[up_place(s[0] ^ k, half)]
        if k == 0:
            keep[...] = part
            keep_up[...] = up_piece
        else:
            out[k - 1][:RANK, :] = part.astype(BF16)
            out[k - 1][RANK:, :] = up_piece.astype(BF16)


def down_pieces(s, n, half, d_low, d_low_got, up_grad, up_got, raw):
    return call(
        functools.partial(down_kernel, n, half),
        [((RANK, half), F32), ((UP_ROWS, half), F32)] + [((RANK + UP_ROWS, half), BF16)] * (n - 1),
        s, [*raw, d_low, d_low_got, up_grad, up_got],
        scratch=[pltpu.VMEM((RANK, VALUE_WIDTH), F32)], flops=1e9,
    )


def update_kernel(s, refs, outs, scratch):
    keep, keep_up, down_ref, up_ref, *got = refs
    fresh, message = outs
    half = fresh.shape[1]
    old_down = down_ref[:, lanes_at(s[1] * half, half)]
    old_up = up_ref[up_place(s[0], half)]
    total, total_up = keep[...], keep_up[...]
    for piece in got:
        total += piece[:RANK, :].astype(F32)
        total_up += piece[RANK:, :].astype(F32)
    new_down = old_down - rate_down * total
    new_up = old_up - rate_up * total_up
    high = new_up.astype(BF16)
    fresh[...] = new_down
    message[:RANK, :] = new_down.astype(BF16)
    message[RANK : RANK + UP_ROWS, :] = high
    message[RANK + UP_ROWS :, :] = (new_up - high.astype(F32)).astype(BF16)


def update(s, keep, keep_up, down_t, up, got):
    half = keep.shape[1]
    return call(
        update_kernel,
        [((RANK, half), F32), ((RANK + 2 * UP_ROWS, half), BF16)],
        s, [keep, keep_up, down_t, up, *got],
    )


def score_low_kernel(n, half, s, refs, outs, scratch):
    xs, xso, *messages = refs
    mine, other, up = outs
    low_mine = low_other = None
    for k in range(n):
        here = lanes_at((s[0] ^ k) * 2 * half + s[1] * half, half)
        message = messages[k]
        part = dot_nt(xs[:, here], message[:RANK, :])
        low_mine = part if low_mine is None else low_mine + part
        part = dot_nt(xso[:, here], message[:RANK, :])
        low_other = part if low_other is None else low_other + part
        high = message[RANK : RANK + UP_ROWS, :].astype(F32)
        up[up_place(s[0] ^ k, half)] = high + message[RANK + UP_ROWS :, :].astype(F32)
    mine[...] = low_mine
    other[...] = low_other


def score_low(s, half, messages, raw):
    n, u = len(messages), raw[0].shape[0]
    return call(
        functools.partial(score_low_kernel, n, half),
        [((u, RANK), F32), ((u, RANK), F32), ((RANK, VALUE_WIDTH), F32)],
        s, [*raw, *messages], flops=2e8,
    )


def score_kernel(s, refs, outs, scratch):
    base, mine, got, up, probs, fresh, fresh_got = refs
    out, new_down, new_up = outs
    half = new_down.shape[1] // 2
    low = (mine[...] + got[...]).astype(BF16)
    u = low.shape[0]
    values = base[...] + adapter_scale_factor * dot_nn(low, up[...].astype(BF16))
    values = values.astype(BF16)
    for g in range(KV_HEADS):
        attended = dot_nn(probs[g], values[:, g * HEAD_DIM : (g + 1) * HEAD_DIM]).astype(BF16)
        for j in range(GROUP):
            h = g * GROUP + j
            out[:, h * HEAD_DIM : (h + 1) * HEAD_DIM] = attended[j * u : (j + 1) * u, :]
    new_down[:, lanes_at(s[1] * half, half)] = fresh[...]
    new_down[:, lanes_at((1 - s[1]) * half, half)] = fresh_got[...]
    new_up[...] = up[...]


def score(s, base, mine, got, up, probs, fresh, fresh_got):
    u, half = base.shape[0], fresh.shape[1]
    return call(
        score_kernel,
        [((u, Q_HEADS * HEAD_DIM), BF16), ((RANK, 2 * half), F32), (up.shape, F32)],
        s, [base, mine, got, up, probs, fresh, fresh_got], flops=2e8, final=(0, 1, 2),
    )


def reduce_order(n):
    return [*range(n - 2, 0, -2), *range(n - 1, 0, -2)]


def solution(mesh):
    n_fsdp, n_view = mesh.shape["fsdp"], mesh.shape["view"]
    line = n_fsdp // 2

    def ring_device(place):
        place = place % n_fsdp
        return 2 * place if place < line else 2 * (n_fsdp - 1 - place) + 1

    forward = [(ring_device(i), ring_device(i + 1)) for i in range(n_fsdp)]
    backward = [(b, a) for a, b in forward]

    def over_view(array, bit):
        return lax.ppermute(array, "view", [(i, i ^ bit) for i in range(n_view)])

    def swap(array):
        return lax.ppermute(array, "view", [(i, i ^ 1) for i in range(n_view)])

    def exchange(array, k):
        return lax.ppermute(array, "fsdp", [(i, i ^ k) for i in range(n_fsdp)])

    def body(
        train_input,
        train_query,
        train_keys,
        train_target,
        train_segments,
        value_weight,
        adapter_down,
        adapter_up,
        score_input,
        score_query,
        score_keys,
        score_segments,
    ):
        width = train_input.shape[-1]
        x = train_input.reshape(-1, width)
        xs = score_input.reshape(-1, width)
        query, keyset, target = (a.reshape(x.shape[0], -1) for a in (train_query, train_keys, train_target))
        squery, skeyset = (a.reshape(xs.shape[0], -1) for a in (score_query, score_keys))
        shard = value_weight.shape[0]
        half = shard // 2
        me = lax.axis_index("fsdp")
        core = lax.axis_index("view") % 2
        place = jnp.where(me % 2 == 0, me // 2, n_fsdp - 1 - me // 2)
        s = jnp.stack([me, core, place]).astype(jnp.int32)

        down_t = adapter_down.T
        down_half = down_t.astype(BF16)
        my_down = lax.dynamic_slice_in_dim(down_half, core * half, half, 1)
        my_weight = lax.dynamic_slice_in_dim(value_weight, core * half, half, 0)
        pieces = [
            jnp.concatenate(
                [
                    my_weight[q * half // 2 : (q + 1) * half // 2],
                    pack_down(my_down[q * RANK // 2 : (q + 1) * RANK // 2], half),
                ],
                axis=0,
            )
            for q in range(2)
        ]

        seg_row, seg_col = train_segments.reshape(1, -1), train_segments.reshape(-1, 1)
        sseg_row, sseg_col = score_segments.reshape(1, -1), score_segments.reshape(-1, 1)
        near_query, near_keys, near_target = near(query), near(keyset), near(target)

        def head(g, deps):
            return train_head(s, g, seg_row, seg_col, near_query, near_keys, near_target, deps)

        def onward(array, ahead):
            return lax.ppermute(array, "fsdp", forward if ahead else backward)

        steps = n_fsdp // 2
        arrived, offsets = list(pieces), [0]
        ahead, back = list(pieces), list(pieces)
        heads = [None] * KV_HEADS
        for k in range(1, steps + 1):
            if k < steps:
                for q in range(2):
                    ahead[q] = onward(ahead[q], True)
                    back[q] = onward(back[q], False)
            else:
                last = [onward(ahead[0], True), onward(back[1], False)]
            if k == 1:
                xo, xso = swap(x), swap(xs)
                raw = tuple(near(a) for a in (x, xo, xs, xso))
                heads[0] = head(0, ())
                probs = score_probs(s, sseg_row, sseg_col, squery, skeyset, ())
            elif k == 2:
                heads[1] = head(1, ())
                heads[2] = head(2, ())
            elif k == 3:
                partial = project(s, n_fsdp, offsets, half, arrived, (), raw, False)
                cut = len(offsets)
            if k < steps:
                arrived += [*ahead, *back]
                offsets += [n_fsdp - k, k]
        sums, sums_out = project(s, n_fsdp, offsets[cut:], half, arrived[2 * cut :], partial, raw, True)
        sums_got = swap(sums_out)
        heads[3] = head(3, ())
        last += [swap(a) for a in last]
        base, d_low, up_grad = value_grads(
            s, n_fsdp, steps, half, last, sums, sums_got, adapter_up, heads, (raw[0], raw[2])
        )
        d_low_got, up_got = swap(d_low), swap(up_grad)
        keep, keep_up, *out = down_pieces(s, n_fsdp, half, d_low, d_low_got, up_grad, up_got, raw[:2])
        bit = 2
        while bit < n_view:
            keep, keep_up = (a + over_view(a, bit) for a in (keep, keep_up))
            out = [(a.astype(F32) + over_view(a, bit).astype(F32)).astype(BF16) for a in out]
            bit *= 2

        got = [None] * len(out)
        for k in reduce_order(n_fsdp):
            got[k - 1] = exchange(out[k - 1], k)
        fresh, message = update(s, keep, keep_up, down_t, adapter_up, got)
        messages = [message] + [None] * (n_fsdp - 1)
        for k in range(n_fsdp - 2, 0, -2):
            messages[k] = exchange(message, k)
        for k in range(0, n_fsdp, 2):
            messages[k + 1] = exchange(messages[k], 1)
        fresh_got = swap(fresh)
        mine, other, new_up = score_low(s, half, messages, raw[2:])
        other_got = swap(other)
        scored, new_down, new_up = score(s, base, mine, other_got, new_up, probs, fresh, fresh_got)
        return (new_down.T, new_up, scored.reshape(score_query.shape))

    in_specs = (
        P(("task", "view"), "fsdp", None),
        P(("task", "view"), "fsdp", None),
        P(("task", "view"), "fsdp", None),
        P(("task", "view"), "fsdp", None),
        P(("task", "view"), "fsdp", None),
        P("fsdp", None),
        P(("task", "fsdp"), None),
        P("task", None),
        P(("task", "view"), "fsdp", None),
        P(("task", "view"), "fsdp", None),
        P(("task", "view"), "fsdp", None),
        P(("task", "view"), "fsdp", None),
    )
    out_specs = (P(("task", "fsdp"), None), P("task", None), P(("task", "view"), "fsdp", None))
    return jax.shard_map(body, mesh=mesh, in_specs=in_specs, out_specs=out_specs, check_vma=False)
```

```python
import functools

import jax
import jax.numpy as jnp
from jax import lax
from jax.experimental import pallas as pl
from jax.experimental.pallas import tpu as pltpu
from jax.sharding import PartitionSpec as P


Q_HEADS = 32
KV_HEADS = 4
HEAD_DIM = 128
GROUP = 8
VALUE_WIDTH = 512
RANK = 64
UP_ROWS = 8

adapter_scale_factor = 0.5
rate_down = 2e-05
rate_up = 0.001


F32 = jnp.float32
BF16 = jnp.bfloat16
VM = pl.BlockSpec(memory_space=pltpu.VMEM)
SM = pl.BlockSpec(memory_space=pltpu.SMEM)
ANY = pl.BlockSpec(memory_space=pl.ANY)
HBM = pl.BlockSpec(memory_space=pltpu.MemorySpace.HBM)
VMEM_GRANT = 16 * 2**20


def dot_nn(a, b):
    return lax.dot_general(a, b, (((1,), (0,)), ((), ())), preferred_element_type=F32)


def dot_nt(a, b):
    return lax.dot_general(a, b, (((1,), (1,)), ((), ())), preferred_element_type=F32)


def cost(flops, nbytes):
    return pl.CostEstimate(flops=int(flops), bytes_accessed=int(nbytes), transcendentals=0)


def near(array):
    return pltpu.with_memory_space_constraint(array, pltpu.VMEM)


def far_off(array):
    return pltpu.with_memory_space_constraint(array, pltpu.MemorySpace.HBM)


def touch(s, arrays):
    def kernel(s, refs, outs, scratch):
        outs[0][...] = jnp.zeros_like(outs[0])

    return call(kernel, [((8, 128), F32)], s, arrays)


def call(kernel, outs, scalars, operands, scratch=(), flops=1e6, final=(), deps=()):
    n, d = len(operands), len(deps)

    def whole(scalar_ref, *refs):
        kernel(scalar_ref, refs[:n], refs[n + d : n + d + len(outs)], refs[n + d + len(outs) :])

    return pl.pallas_call(
        whole,
        out_shape=[jax.ShapeDtypeStruct(*o) if i in final else pltpu.VMEM(*o) for i, o in enumerate(outs)],
        in_specs=[SM] + [VM] * n + [ANY] * d,
        out_specs=[VM] * len(outs),
        scratch_shapes=list(scratch),
        cost_estimate=cost(flops, 2**20),
        compiler_params=pltpu.CompilerParams(vmem_limit_bytes=VMEM_GRANT),
    )(scalars, *[near(a) for a in operands], *deps)


def lanes_at(start, size):
    return pl.ds(pl.multiple_of(start, 128), size)


def same_segment(seg_row):
    length = seg_row.shape[1]
    across = jnp.broadcast_to(seg_row[...].astype(F32), (length, length))
    return across == across.T


def train_head_kernel(g, s, refs, outs, scratch):
    seg_row, q_ref, k_ref, t_ref = refs
    high_out, rest_out, aimed_out = outs
    length = k_ref.shape[0]
    keys = k_ref[:, g * HEAD_DIM : (g + 1) * HEAD_DIM]
    row = lax.broadcasted_iota(jnp.int32, (length, length), 0)
    col = lax.broadcasted_iota(jnp.int32, (length, length), 1)
    allowed = (row <= col) & same_segment(seg_row)
    lanes = [slice(h * HEAD_DIM, (h + 1) * HEAD_DIM) for h in range(g * GROUP, (g + 1) * GROUP)]
    every = []
    for j in range(GROUP):
        logits = dot_nt(keys, q_ref[:, lanes[j]]) * HEAD_DIM ** (-0.5)
        logits = jnp.where(allowed, logits, -1e30)
        peak = jnp.max(logits, axis=0, keepdims=True)
        weights = jnp.exp(logits - peak)
        every.append((weights / jnp.sum(weights, axis=0, keepdims=True)).astype(BF16))
    gram = sum(dot_nt(probs, probs) for probs in every)
    high = gram.astype(BF16)
    high_out[...] = high
    rest_out[...] = (gram - high.astype(F32)).astype(BF16)
    aimed_out[...] = sum(dot_nn(probs, t_ref[:, lanes[j]]) for j, probs in enumerate(every))


def train_head(s, g, seg_row, query, keyset, target, deps):
    length = query.shape[0]
    return call(
        functools.partial(train_head_kernel, g),
        [((length, length), BF16), ((length, length), BF16), ((length, HEAD_DIM), F32)],
        s, [seg_row, query, keyset, target], flops=2e9, deps=deps,
    )


def score_probs_kernel(s, refs, outs, scratch):
    seg_row, q_ref, k_ref = refs
    (p_ref,) = outs
    length = k_ref.shape[0]
    row = lax.broadcasted_iota(jnp.int32, (length, length), 0)
    col = lax.broadcasted_iota(jnp.int32, (length, length), 1)
    allowed = (col <= row) & same_segment(seg_row)
    for g in range(KV_HEADS):
        keys = k_ref[:, g * HEAD_DIM : (g + 1) * HEAD_DIM]
        for j in range(GROUP):
            h = g * GROUP + j
            logits = dot_nt(q_ref[:, h * HEAD_DIM : (h + 1) * HEAD_DIM], keys) * HEAD_DIM ** (-0.5)
            logits = jnp.where(allowed, logits, -1e30)
            weights = jnp.exp(logits - jnp.max(logits, axis=1, keepdims=True))
            probs = weights / jnp.sum(weights, axis=1, keepdims=True)
            p_ref[g, j * length : (j + 1) * length, :] = probs.astype(BF16)


def score_probs(s, seg_row, query, keyset, deps):
    length = query.shape[0]
    return call(
        score_probs_kernel, [((KV_HEADS, GROUP * length, length), BF16)],
        s, [seg_row, query, keyset], flops=1e9, deps=deps,
    )[0]


def apart(half):
    return half * 5 // 16


def unpack_down(packed, half):
    parts = VALUE_WIDTH // half
    if parts == 1:
        return packed
    return jnp.concatenate([packed[:, i * half : (i + 1) * half] for i in range(parts)], axis=0)


def pack_down(block, half):
    parts = VALUE_WIDTH // half
    if parts == 1:
        return block
    rows = block.shape[0] // parts
    return jnp.concatenate([block[i * rows : (i + 1) * rows] for i in range(parts)], axis=1)


def assemble(s, half, a, y, c, buffer):
    rows = apart(half)
    buffer[pl.ds(pl.multiple_of(s[3] * rows, 16), rows), :] = a[...]
    buffer[pl.ds(pl.multiple_of((1 - s[3]) * rows, 16), rows), :] = y[...]
    buffer[2 * rows :, :] = c[: half - 2 * rows, :]
    return unpack_down(c[half - 2 * rows :, :], half)


def prepare_kernel(half, w_hbm, d_hbm, a, y, c, down, sems):
    core, task = lax.axis_index("view") % 2, lax.axis_index("task") % 2
    rows = apart(half)
    rest = half - 2 * rows

    def weight_rows(start, count):
        return w_hbm.at[pl.ds(pl.multiple_of(core * half + start, 16), count), :]

    copies = [
        pltpu.make_async_copy(weight_rows(task * rows, rows), a, sems.at[0]),
        pltpu.make_async_copy(weight_rows((1 - task) * rows, rows), y, sems.at[1]),
        pltpu.make_async_copy(weight_rows(2 * rows, rest), c.at[pl.ds(0, rest), :], sems.at[2]),
        pltpu.make_async_copy(d_hbm.at[:, lanes_at(core * half, half)], down, sems.at[3]),
    ]
    for copy in copies:
        copy.start()
    copies[3].wait()
    c[rest:, :] = pack_down(down[...].astype(BF16), half)
    for copy in copies[:3]:
        copy.wait()


def prepare(weight, down_t):
    half = weight.shape[0] // 2
    rows = apart(half)
    sizes = (rows, rows, half - 2 * rows + RANK * half // VALUE_WIDTH)
    return pl.pallas_call(
        functools.partial(prepare_kernel, half),
        out_shape=[pltpu.VMEM((size, VALUE_WIDTH), BF16) for size in sizes],
        in_specs=[HBM, HBM],
        out_specs=[VM] * 3,
        scratch_shapes=[pltpu.VMEM((RANK, half), F32), pltpu.SemaphoreType.DMA((4,))],
        cost_estimate=cost(1e6, 2**20),
        compiler_params=pltpu.CompilerParams(vmem_limit_bytes=VMEM_GRANT),
        name="prepare",
    )(far_off(weight), far_off(down_t))


def owner_of(position, n):
    position = lax.rem(position, n)
    return jnp.where(position < n // 2, 2 * position, 2 * (n - 1 - position) + 1)


def fetch_kernel(n, half, s, refs, outs, scratch):
    (sems,) = scratch
    copies = []
    for i, (source, out) in enumerate(zip(refs, outs)):
        for j in range(n):
            here = lanes_at(2 * half * j + (1 - s[1]) * half, half)
            copies.append(
                pltpu.make_async_copy(source.at[:, here], out.at[:, pl.ds(j * half, half)], sems.at[i * n + j])
            )
    for copy in copies:
        copy.start()
    for copy in copies:
        copy.wait()


def fetch(s, n, half, arrays):
    def kernel(scalar_ref, *refs):
        m = len(arrays)
        fetch_kernel(n, half, scalar_ref, refs[:m], refs[m : 2 * m], refs[2 * m :])

    return pl.pallas_call(
        kernel,
        out_shape=[pltpu.VMEM((a.shape[0], n * half), BF16) for a in arrays],
        in_specs=[SM] + [HBM] * len(arrays),
        out_specs=[VM] * len(arrays),
        scratch_shapes=[pltpu.SemaphoreType.DMA((len(arrays) * n,))],
        cost_estimate=cost(1e6, 2**21),
        compiler_params=pltpu.CompilerParams(vmem_limit_bytes=VMEM_GRANT),
        name="fetch",
    )(s, *[far_off(a) for a in arrays])


def project_kernel(n, offsets, half, s, refs, outs, scratch):
    x, xo, xs, xso = refs[:4]
    refs = refs[4:]
    xb, wb, db = scratch
    t, u = x.shape[0], xs.shape[0]
    for i, offset in enumerate(offsets):
        owner = owner_of(s[2] + offset, n)
        whole, packed = lanes_at(owner * 2 * half + s[1] * half, half), lanes_at(owner * half, half)
        there = slice(i * half, (i + 1) * half)
        for at, a, here in ((0, x, whole), (t, xo, packed), (2 * t, xs, whole), (2 * t + u, xso, packed)):
            xb[at : at + a.shape[0], there] = a[:, here]
        db[:, there] = assemble(s, half, *refs[3 * i : 3 * i + 3], wb.at[pl.ds(i * half, half), :])
    total = dot_nn(xb[...], wb[...])
    low = dot_nt(db[...], xb[: 2 * t, :])
    before = refs[3 * len(offsets) :]
    if before:
        total = total + before[0][...]
        low = low + before[1][...]
    if outs[0].shape[0] == total.shape[0]:
        outs[0][...] = total
        outs[1][...] = low
        return
    for i, out in enumerate(outs):
        out[:t, :] = total[i * t : (i + 1) * t, :]
        out[t : t + u, :] = total[2 * t + i * u : 2 * t + (i + 1) * u, :]
        part = low[:, i * t : (i + 1) * t]
        out[t + u :, :t] = part[: RANK // 2, :]
        out[t + u :, t : 2 * t] = part[RANK // 2 :, :]


def project(s, n, offsets, half, pieces, before, raw, final):
    t, u = raw[0].shape[0], raw[2].shape[0]
    if final:
        outs = [((t + u + RANK // 2, VALUE_WIDTH), F32)] * 2
    else:
        outs = [((2 * t + 2 * u, VALUE_WIDTH), F32), ((RANK, 2 * t), F32)]
    return call(
        functools.partial(project_kernel, n, offsets, half),
        outs, s, [*raw, *pieces, *before],
        scratch=[
            pltpu.VMEM((2 * t + 2 * u, len(offsets) * half), BF16),
            pltpu.VMEM((len(offsets) * half, VALUE_WIDTH), BF16),
            pltpu.VMEM((RANK, len(offsets) * half), BF16),
        ],
        flops=len(offsets) * 3.4e8,
    )


def grad_kernel(n, offset, half, s, refs, outs, scratch):
    x, xs = refs[:2]
    pieces, (mine, got, up_ref), heads = refs[2:8], refs[8:11], refs[11:]
    base, d_low_out, up_grad = outs
    wb, db = scratch
    t, u = x.shape[0], xs.shape[0]
    total = mine[:t, :] + got[:t, :]
    base_total = mine[t : t + u, :] + got[t : t + u, :]
    packed = mine[t + u :, :] + got[t + u :, :]
    low = jnp.concatenate([packed[:, :t], packed[:, t : 2 * t]], axis=0)
    for i in range(2):
        start = pl.multiple_of((s[1] if i == 0 else 1 - s[1]) * half, half)
        db[:, lanes_at(start, half)] = assemble(s, half, *pieces[3 * i : 3 * i + 3], wb.at[pl.ds(start, half), :])
    here = lanes_at(owner_of(s[2] + offset, n) * 2 * half, 2 * half)
    total = total + dot_nn(x[:, here], wb[...])
    base_total = base_total + dot_nn(xs[:, here], wb[...])
    low = low + dot_nt(db[...], x[:, here])
    base[...] = base_total
    low = low.astype(BF16)
    up_half = up_ref[...].astype(BF16)
    low_rows = low.astype(F32).T.astype(BF16)
    values = (total + adapter_scale_factor * dot_nn(low_rows, up_half)).astype(BF16)
    grads = []
    for g in range(KV_HEADS):
        head = values[:, g * HEAD_DIM : (g + 1) * HEAD_DIM]
        high, rest, aimed = heads[3 * g : 3 * g + 3]
        d_head = dot_nn(high[...], head) + dot_nn(rest[...], head) - aimed[...]
        grads.append(d_head.astype(BF16))
    d_values = jnp.concatenate(grads, axis=1)
    d_low_out[...] = (adapter_scale_factor * dot_nt(up_half, d_values)).astype(BF16)
    up_grad[...] = adapter_scale_factor * dot_nn(low, d_values)


def value_grads(s, n, offset, half, pieces, mine, got, up, heads, raw):
    t, u = raw[0].shape[0], raw[1].shape[0]
    return call(
        functools.partial(grad_kernel, n, offset, half),
        [((u, VALUE_WIDTH), F32), ((RANK, t), BF16), ((RANK, VALUE_WIDTH), F32)],
        s, [*raw, *pieces, mine, got, up, *[a for h in heads for a in h]],
        scratch=[pltpu.VMEM((2 * half, VALUE_WIDTH), BF16), pltpu.VMEM((RANK, 2 * half), BF16)], flops=1e9,
    )


def up_place(device, half):
    columns = VALUE_WIDTH // half
    row = pl.multiple_of(lax.div(device, columns) * UP_ROWS, UP_ROWS)
    col = lax.rem(device, columns) * half
    return pl.ds(row, UP_ROWS), lanes_at(col, half)


def down_kernel(chosen, half, s, refs, outs, scratch):
    x, xo, d_low, d_low_got, up_grad, up_got = refs
    (up_sum,) = scratch
    outs = list(outs)
    up_sum[...] = up_grad[...] + up_got[...]
    for k in chosen:
        here, packed = lanes_at((s[0] ^ k) * 2 * half + s[1] * half, half), lanes_at((s[0] ^ k) * half, half)
        part = dot_nn(d_low[...], x[:, here]) + dot_nn(d_low_got[...], xo[:, packed])
        up_piece = up_sum[up_place(s[0] ^ k, half)]
        if k == 0:
            outs.pop(0)[...] = part
            outs.pop(0)[...] = up_piece
        else:
            out = outs.pop(0)
            out[:RANK, :] = part.astype(BF16)
            out[RANK:, :] = up_piece.astype(BF16)


def down_pieces(s, chosen, half, d_low, d_low_got, up_grad, up_got, raw):
    keep = [((RANK, half), F32), ((UP_ROWS, half), F32)]
    return call(
        functools.partial(down_kernel, chosen, half),
        [o for k in chosen for o in (keep if k == 0 else [((RANK + UP_ROWS, half), BF16)])],
        s, [*raw, d_low, d_low_got, up_grad, up_got],
        scratch=[pltpu.VMEM((RANK, VALUE_WIDTH), F32)], flops=1e9,
    )


def update_kernel(s, refs, outs, scratch):
    keep, keep_up, down_ref, up_ref, *got = refs
    fresh, message = outs
    half = fresh.shape[1]
    old_down = down_ref[:, lanes_at(s[1] * half, half)]
    old_up = up_ref[up_place(s[0], half)]
    total, total_up = keep[...], keep_up[...]
    for piece in got:
        total += piece[:RANK, :].astype(F32)
        total_up += piece[RANK:, :].astype(F32)
    new_down = old_down - rate_down * total
    new_up = old_up - rate_up * total_up
    high = new_up.astype(BF16)
    fresh[...] = new_down
    message[:RANK, :] = new_down.astype(BF16)
    message[RANK : RANK + UP_ROWS, :] = high
    message[RANK + UP_ROWS :, :] = (new_up - high.astype(F32)).astype(BF16)


def update(s, keep, keep_up, down_t, up, got):
    half = keep.shape[1]
    return call(
        update_kernel,
        [((RANK, half), F32), ((RANK + 2 * UP_ROWS, half), BF16)],
        s, [keep, keep_up, down_t, up, *got],
    )


def score_low_kernel(n, half, s, refs, outs, scratch):
    xs, xso, *messages = refs
    mine, other, up = outs
    low_mine = low_other = None
    for k in range(n):
        here = lanes_at((s[0] ^ k) * 2 * half + s[1] * half, half)
        message = messages[k]
        part = dot_nt(xs[:, here], message[:RANK, :])
        low_mine = part if low_mine is None else low_mine + part
        part = dot_nt(xso[:, lanes_at((s[0] ^ k) * half, half)], message[:RANK, :])
        low_other = part if low_other is None else low_other + part
        high = message[RANK : RANK + UP_ROWS, :].astype(F32)
        up[up_place(s[0] ^ k, half)] = high + message[RANK + UP_ROWS :, :].astype(F32)
    mine[...] = low_mine
    other[...] = low_other


def score_low(s, half, messages, raw):
    n, u = len(messages), raw[0].shape[0]
    return call(
        functools.partial(score_low_kernel, n, half),
        [((u, RANK), F32), ((u, RANK), F32), ((RANK, VALUE_WIDTH), F32)],
        s, [*raw, *messages], flops=2e8,
    )


def score_kernel(s, refs, outs, scratch):
    base, mine, got, up, probs, fresh, fresh_got = refs
    out, new_down, new_up = outs
    half = new_down.shape[1] // 2
    low = (mine[...] + got[...]).astype(BF16)
    u = low.shape[0]
    values = base[...] + adapter_scale_factor * dot_nn(low, up[...].astype(BF16))
    values = values.astype(BF16)
    for g in range(KV_HEADS):
        attended = dot_nn(probs[g], values[:, g * HEAD_DIM : (g + 1) * HEAD_DIM]).astype(BF16)
        for j in range(GROUP):
            h = g * GROUP + j
            out[:, h * HEAD_DIM : (h + 1) * HEAD_DIM] = attended[j * u : (j + 1) * u, :]
    new_down[:, lanes_at(s[1] * half, half)] = fresh[...]
    new_down[:, lanes_at((1 - s[1]) * half, half)] = fresh_got[...]
    new_up[...] = up[...]


def score(s, base, mine, got, up, probs, fresh, fresh_got):
    u, half = base.shape[0], fresh.shape[1]
    return call(
        score_kernel,
        [((u, Q_HEADS * HEAD_DIM), BF16), ((RANK, 2 * half), F32), (up.shape, F32)],
        s, [base, mine, got, up, probs, fresh, fresh_got], flops=2e8, final=(0, 1, 2),
    )


def reduce_order(n):
    far = [*range(n - 2, n // 2 - 1, -2), *range(n - 1, n // 2, -2)]
    near_by = [*range(n // 2 - 1, 0, -1)]
    return far, near_by


def solution(mesh):
    n_fsdp, n_view, n_task = mesh.shape["fsdp"], mesh.shape["view"], mesh.shape["task"]
    line = n_fsdp // 2

    def ring_device(place):
        place = place % n_fsdp
        return 2 * place if place < line else 2 * (n_fsdp - 1 - place) + 1

    forward = [(ring_device(i), ring_device(i + 1)) for i in range(n_fsdp)]
    backward = [(b, a) for a, b in forward]

    def over_view(array, bit):
        return lax.ppermute(array, "view", [(i, i ^ bit) for i in range(n_view)])

    def swap(array):
        return lax.ppermute(array, "view", [(i, i ^ 1) for i in range(n_view)])

    def exchange(array, k):
        return lax.ppermute(array, "fsdp", [(i, i ^ k) for i in range(n_fsdp)])

    def body(
        train_input,
        train_query,
        train_keys,
        train_target,
        train_segments,
        value_weight,
        adapter_down,
        adapter_up,
        score_input,
        score_query,
        score_keys,
        score_segments,
    ):
        width = train_input.shape[-1]
        x = train_input.reshape(-1, width)
        xs = score_input.reshape(-1, width)
        query, keyset, target = (a.reshape(x.shape[0], -1) for a in (train_query, train_keys, train_target))
        squery, skeyset = (a.reshape(xs.shape[0], -1) for a in (score_query, score_keys))
        shard = value_weight.shape[0]
        half = shard // 2
        me = lax.axis_index("fsdp")
        core = lax.axis_index("view") % 2
        place = jnp.where(me % 2 == 0, me // 2, n_fsdp - 1 - me // 2)
        s = jnp.stack([me, core, place, lax.axis_index("task") % 2]).astype(jnp.int32)

        down_t = adapter_down.T
        a_piece, y_piece, c_piece = prepare(value_weight, down_t)

        seg_row, sseg_row = train_segments.reshape(1, -1), score_segments.reshape(1, -1)
        near_query, near_keys, near_target = near(query), near(keyset), near(target)

        def head(g, deps):
            return train_head(s, g, seg_row, near_query, near_keys, near_target, deps)

        def onward(array, ahead):
            return lax.ppermute(array, "fsdp", forward if ahead else backward)

        def over_task(array):
            return lax.ppermute(array, "task", [(i, i ^ 1) for i in range(n_task)])

        steps = n_fsdp // 2
        arrived, offsets = [a_piece, y_piece, c_piece], [0]
        a_ahead = a_back = a_piece
        c_ahead = c_back = c_piece
        heads = [None] * KV_HEADS
        for k in range(1, steps):
            a_ahead, a_back = onward(a_ahead, True), onward(a_back, False)
            c_ahead, c_back = onward(c_ahead, True), onward(c_back, False)
            if k == 1:
                xo, xso = fetch(s, n_fsdp, half, (x, xs))
                xo, xso = swap(xo), swap(xso)
                raw = tuple(near(a) for a in (x, xo, xs, xso))
                touched = touch(s, (near_query, near_keys, near_target, seg_row))[0]
                heads[0] = head(0, (touched,))
                probs = score_probs(s, sseg_row, squery, skeyset, ())
            elif k == 2:
                heads[1] = head(1, ())
                heads[2] = head(2, ())
            elif k == 3:
                partial = project(s, n_fsdp, offsets, half, arrived, (), raw, False)
                cut = len(offsets)
            arrived += [a_ahead, over_task(a_ahead), c_ahead]
            arrived += [a_back, over_task(a_back), c_back]
            offsets += [n_fsdp - k, k]
        a_last, c_last = onward(a_ahead, True), onward(c_back, False)
        last = [a_last, over_task(a_last), c_last]
        heads[3] = head(3, ())
        sums, sums_out = project(s, n_fsdp, offsets[cut:], half, arrived[3 * cut :], partial, raw, True)
        sums_got = swap(sums_out)
        last += [swap(a) for a in last]
        base, d_low, up_grad = value_grads(
            s, n_fsdp, steps, half, last, sums, sums_got, adapter_up, heads, (raw[0], raw[2])
        )
        d_low_got, up_got = swap(d_low), swap(up_grad)
        far, near_by = reduce_order(n_fsdp)
        out = [None] * (n_fsdp - 1)

        def pieces_of(chosen):
            return down_pieces(s, chosen, half, d_low, d_low_got, up_grad, up_got, raw[:2])

        for k, array in zip(far, pieces_of(far)):
            out[k - 1] = array
        *some, keep, keep_up = pieces_of([*near_by, 0])
        for k, array in zip(near_by, some):
            out[k - 1] = array
        bit = 2
        while bit < n_view:
            keep, keep_up = (a + over_view(a, bit) for a in (keep, keep_up))
            out = [(a.astype(F32) + over_view(a, bit).astype(F32)).astype(BF16) for a in out]
            bit *= 2

        got = [None] * len(out)
        for k in far + near_by:
            got[k - 1] = exchange(out[k - 1], k)
        fresh, message = update(s, keep, keep_up, down_t, adapter_up, got)
        messages = [message] + [None] * (n_fsdp - 1)
        for k in range(n_fsdp - 2, 0, -2):
            messages[k] = exchange(message, k)
        for k in range(0, n_fsdp, 2):
            messages[k + 1] = exchange(messages[k], 1)
        fresh_got = swap(fresh)
        mine, other, new_up = score_low(s, half, messages, raw[2:])
        other_got = swap(other)
        scored, new_down, new_up = score(s, base, mine, other_got, new_up, probs, fresh, fresh_got)
        return (new_down.T, new_up, scored.reshape(score_query.shape))

    in_specs = (
        P(("task", "view"), "fsdp", None),
        P(("task", "view"), "fsdp", None),
        P(("task", "view"), "fsdp", None),
        P(("task", "view"), "fsdp", None),
        P(("task", "view"), "fsdp", None),
        P("fsdp", None),
        P(("task", "fsdp"), None),
        P("task", None),
        P(("task", "view"), "fsdp", None),
        P(("task", "view"), "fsdp", None),
        P(("task", "view"), "fsdp", None),
        P(("task", "view"), "fsdp", None),
    )
    out_specs = (P(("task", "fsdp"), None), P("task", None), P(("task", "view"), "fsdp", None))
    return jax.shard_map(body, mesh=mesh, in_specs=in_specs, out_specs=out_specs, check_vma=False)
```

```python
import functools

import jax
import jax.numpy as jnp
from jax import lax
from jax.experimental import pallas as pl
from jax.experimental.pallas import tpu as pltpu
from jax.sharding import PartitionSpec as P


Q_HEADS = 32
KV_HEADS = 4
HEAD_DIM = 128
GROUP = 8
VALUE_WIDTH = 512
RANK = 64
UP_ROWS = 8

adapter_scale_factor = 0.5
rate_down = 2e-05
rate_up = 0.001


F32 = jnp.float32
BF16 = jnp.bfloat16
VM = pl.BlockSpec(memory_space=pltpu.VMEM)
SM = pl.BlockSpec(memory_space=pltpu.SMEM)
ANY = pl.BlockSpec(memory_space=pl.ANY)
HBM = pl.BlockSpec(memory_space=pltpu.MemorySpace.HBM)
VMEM_GRANT = 16 * 2**20


def dot_nn(a, b):
    return lax.dot_general(a, b, (((1,), (0,)), ((), ())), preferred_element_type=F32)


def dot_nt(a, b):
    return lax.dot_general(a, b, (((1,), (1,)), ((), ())), preferred_element_type=F32)


def cost(flops, nbytes):
    return pl.CostEstimate(flops=int(flops), bytes_accessed=int(nbytes), transcendentals=0)


def near(array):
    return pltpu.with_memory_space_constraint(array, pltpu.VMEM)


def far_off(array):
    return pltpu.with_memory_space_constraint(array, pltpu.MemorySpace.HBM)


def touch(s, arrays):
    def kernel(s, refs, outs, scratch):
        outs[0][...] = jnp.zeros_like(outs[0])

    return call(kernel, [((8, 128), F32)], s, arrays)


def call(kernel, outs, scalars, operands, scratch=(), flops=1e6, final=(), deps=()):
    n, d = len(operands), len(deps)

    def whole(scalar_ref, *refs):
        kernel(scalar_ref, refs[:n], refs[n + d : n + d + len(outs)], refs[n + d + len(outs) :])

    return pl.pallas_call(
        whole,
        out_shape=[jax.ShapeDtypeStruct(*o) if i in final else pltpu.VMEM(*o) for i, o in enumerate(outs)],
        in_specs=[SM] + [VM] * n + [ANY] * d,
        out_specs=[VM] * len(outs),
        scratch_shapes=list(scratch),
        cost_estimate=cost(flops, 2**20),
        compiler_params=pltpu.CompilerParams(vmem_limit_bytes=VMEM_GRANT),
    )(scalars, *[near(a) for a in operands], *deps)


def lanes_at(start, size):
    return pl.ds(pl.multiple_of(start, 128), size)


def same_segment(seg_row):
    length = seg_row.shape[1]
    across = jnp.broadcast_to(seg_row[...].astype(F32), (length, length))
    return across == across.T


def train_head_kernel(g, s, refs, outs, scratch):
    seg_row, q_ref, k_ref, t_ref = refs
    high_out, rest_out, aimed_out = outs
    length = k_ref.shape[0]
    keys = k_ref[:, g * HEAD_DIM : (g + 1) * HEAD_DIM]
    row = lax.broadcasted_iota(jnp.int32, (length, length), 0)
    col = lax.broadcasted_iota(jnp.int32, (length, length), 1)
    allowed = (row <= col) & same_segment(seg_row)
    lanes = [slice(h * HEAD_DIM, (h + 1) * HEAD_DIM) for h in range(g * GROUP, (g + 1) * GROUP)]
    every = []
    for j in range(GROUP):
        logits = dot_nt(keys, q_ref[:, lanes[j]]) * HEAD_DIM ** (-0.5)
        logits = jnp.where(allowed, logits, -1e30)
        peak = jnp.max(logits, axis=0, keepdims=True)
        weights = jnp.exp(logits - peak)
        every.append((weights * (1.0 / jnp.sum(weights, axis=0, keepdims=True))).astype(BF16))
    gram = sum(dot_nt(probs, probs) for probs in every)
    high = gram.astype(BF16)
    high_out[...] = high
    rest_out[...] = (gram - high.astype(F32)).astype(BF16)
    aimed_out[...] = sum(dot_nn(probs, t_ref[:, lanes[j]]) for j, probs in enumerate(every))


def train_head(s, g, seg_row, query, keyset, target, deps):
    length = query.shape[0]
    return call(
        functools.partial(train_head_kernel, g),
        [((length, length), BF16), ((length, length), BF16), ((length, HEAD_DIM), F32)],
        s, [seg_row, query, keyset, target], flops=2e9, deps=deps,
    )


def score_probs_kernel(s, refs, outs, scratch):
    seg_row, q_ref, k_ref = refs
    (p_ref,) = outs
    length = k_ref.shape[0]
    row = lax.broadcasted_iota(jnp.int32, (length, length), 0)
    col = lax.broadcasted_iota(jnp.int32, (length, length), 1)
    allowed = (col <= row) & same_segment(seg_row)
    for g in range(KV_HEADS):
        keys = k_ref[:, g * HEAD_DIM : (g + 1) * HEAD_DIM]
        for j in range(GROUP):
            h = g * GROUP + j
            logits = dot_nt(q_ref[:, h * HEAD_DIM : (h + 1) * HEAD_DIM], keys) * HEAD_DIM ** (-0.5)
            logits = jnp.where(allowed, logits, -1e30)
            weights = jnp.exp(logits - jnp.max(logits, axis=1, keepdims=True))
            probs = weights / jnp.sum(weights, axis=1, keepdims=True)
            p_ref[g, j * length : (j + 1) * length, :] = probs.astype(BF16)


def score_probs(s, seg_row, query, keyset, deps):
    length = query.shape[0]
    return call(
        score_probs_kernel, [((KV_HEADS, GROUP * length, length), BF16)],
        s, [seg_row, query, keyset], flops=1e9, deps=deps,
    )[0]


def apart(half):
    return half * 5 // 16


def unpack_down(packed, half):
    parts = VALUE_WIDTH // half
    if parts == 1:
        return packed
    return jnp.concatenate([packed[:, i * half : (i + 1) * half] for i in range(parts)], axis=0)


def pack_down(block, half):
    parts = VALUE_WIDTH // half
    if parts == 1:
        return block
    rows = block.shape[0] // parts
    return jnp.concatenate([block[i * rows : (i + 1) * rows] for i in range(parts)], axis=1)


def assemble(s, half, a, y, c, buffer):
    rows = apart(half)
    buffer[pl.ds(pl.multiple_of(s[3] * rows, 16), rows), :] = a[...]
    buffer[pl.ds(pl.multiple_of((1 - s[3]) * rows, 16), rows), :] = y[...]
    buffer[2 * rows :, :] = c[: half - 2 * rows, :]
    return unpack_down(c[half - 2 * rows :, :], half)


def prepare_kernel(half, w_hbm, d_hbm, a, y, c, down, sems):
    core, task = lax.axis_index("view") % 2, lax.axis_index("task") % 2
    rows = apart(half)
    rest = half - 2 * rows

    def weight_rows(start, count):
        return w_hbm.at[pl.ds(pl.multiple_of(core * half + start, 16), count), :]

    copies = [
        pltpu.make_async_copy(weight_rows(task * rows, rows), a, sems.at[0]),
        pltpu.make_async_copy(weight_rows((1 - task) * rows, rows), y, sems.at[1]),
        pltpu.make_async_copy(weight_rows(2 * rows, rest), c.at[pl.ds(0, rest), :], sems.at[2]),
        pltpu.make_async_copy(d_hbm.at[:, lanes_at(core * half, half)], down, sems.at[3]),
    ]
    for copy in copies:
        copy.start()
    copies[3].wait()
    c[rest:, :] = pack_down(down[...].astype(BF16), half)
    for copy in copies[:3]:
        copy.wait()


def prepare(weight, down_t):
    half = weight.shape[0] // 2
    rows = apart(half)
    sizes = (rows, rows, half - 2 * rows + RANK * half // VALUE_WIDTH)
    return pl.pallas_call(
        functools.partial(prepare_kernel, half),
        out_shape=[pltpu.VMEM((size, VALUE_WIDTH), BF16) for size in sizes],
        in_specs=[HBM, HBM],
        out_specs=[VM] * 3,
        scratch_shapes=[pltpu.VMEM((RANK, half), F32), pltpu.SemaphoreType.DMA((4,))],
        cost_estimate=cost(1e6, 2**20),
        compiler_params=pltpu.CompilerParams(vmem_limit_bytes=VMEM_GRANT),
    )(far_off(weight), far_off(down_t))


def owner_of(position, n):
    position = lax.rem(position, n)
    return jnp.where(position < n // 2, 2 * position, 2 * (n - 1 - position) + 1)


def fetch_kernel(n, half, s, refs, outs, scratch):
    (sems,) = scratch
    copies = []
    for i, (source, out) in enumerate(zip(refs, outs)):
        for j in range(n):
            here = lanes_at(2 * half * j + (1 - s[1]) * half, half)
            copies.append(
                pltpu.make_async_copy(source.at[:, here], out.at[:, pl.ds(j * half, half)], sems.at[i * n + j])
            )
    for copy in copies:
        copy.start()
    for copy in copies:
        copy.wait()


def fetch(s, n, half, arrays):
    def kernel(scalar_ref, *refs):
        m = len(arrays)
        fetch_kernel(n, half, scalar_ref, refs[:m], refs[m : 2 * m], refs[2 * m :])

    return pl.pallas_call(
        kernel,
        out_shape=[pltpu.VMEM((a.shape[0], n * half), BF16) for a in arrays],
        in_specs=[SM] + [HBM] * len(arrays),
        out_specs=[VM] * len(arrays),
        scratch_shapes=[pltpu.SemaphoreType.DMA((len(arrays) * n,))],
        cost_estimate=cost(1e6, 2**21),
        compiler_params=pltpu.CompilerParams(vmem_limit_bytes=VMEM_GRANT),
    )(s, *[far_off(a) for a in arrays])


def project_kernel(n, offsets, half, s, refs, outs, scratch):
    x, xo, xs, xso = refs[:4]
    refs = refs[4:]
    xb, wb, db = scratch
    t, u = x.shape[0], xs.shape[0]
    for i, offset in enumerate(offsets):
        owner = owner_of(s[2] + offset, n)
        whole, packed = lanes_at(owner * 2 * half + s[1] * half, half), lanes_at(owner * half, half)
        there = slice(i * half, (i + 1) * half)
        for at, a, here in ((0, x, whole), (t, xo, packed), (2 * t, xs, whole), (2 * t + u, xso, packed)):
            xb[at : at + a.shape[0], there] = a[:, here]
        db[:, there] = assemble(s, half, *refs[3 * i : 3 * i + 3], wb.at[pl.ds(i * half, half), :])
    total = dot_nn(xb[...], wb[...])
    low = dot_nt(db[...], xb[: 2 * t, :])
    before = refs[3 * len(offsets) :]
    if before:
        total = total + before[0][...]
        low = low + before[1][...]
    if outs[0].shape[0] == total.shape[0]:
        outs[0][...] = total
        outs[1][...] = low
        return
    for i, out in enumerate(outs):
        out[:t, :] = total[i * t : (i + 1) * t, :]
        out[t : t + u, :] = total[2 * t + i * u : 2 * t + (i + 1) * u, :]
        part = low[:, i * t : (i + 1) * t]
        out[t + u :, :t] = part[: RANK // 2, :]
        out[t + u :, t : 2 * t] = part[RANK // 2 :, :]


def project(s, n, offsets, half, pieces, before, raw, final):
    t, u = raw[0].shape[0], raw[2].shape[0]
    if final:
        outs = [((t + u + RANK // 2, VALUE_WIDTH), F32)] * 2
    else:
        outs = [((2 * t + 2 * u, VALUE_WIDTH), F32), ((RANK, 2 * t), F32)]
    return call(
        functools.partial(project_kernel, n, offsets, half),
        outs, s, [*raw, *pieces, *before],
        scratch=[
            pltpu.VMEM((2 * t + 2 * u, len(offsets) * half), BF16),
            pltpu.VMEM((len(offsets) * half, VALUE_WIDTH), BF16),
            pltpu.VMEM((RANK, len(offsets) * half), BF16),
        ],
        flops=len(offsets) * 3.4e8,
    )


def grad_kernel(n, offset, half, s, refs, outs, scratch):
    x, xs = refs[:2]
    pieces, (mine, got, up_ref), heads = refs[2:8], refs[8:11], refs[11:]
    base, d_low_out, up_grad = outs
    wb, db = scratch
    t, u = x.shape[0], xs.shape[0]
    total = mine[:t, :] + got[:t, :]
    base_total = mine[t : t + u, :] + got[t : t + u, :]
    packed = mine[t + u :, :] + got[t + u :, :]
    low = jnp.concatenate([packed[:, :t], packed[:, t : 2 * t]], axis=0)
    for i in range(2):
        start = pl.multiple_of((s[1] if i == 0 else 1 - s[1]) * half, half)
        db[:, lanes_at(start, half)] = assemble(s, half, *pieces[3 * i : 3 * i + 3], wb.at[pl.ds(start, half), :])
    here = lanes_at(owner_of(s[2] + offset, n) * 2 * half, 2 * half)
    total = total + dot_nn(x[:, here], wb[...])
    base_total = base_total + dot_nn(xs[:, here], wb[...])
    low = low + dot_nt(db[...], x[:, here])
    base[...] = base_total
    low = low.astype(BF16)
    up_half = up_ref[...].astype(BF16)
    low_rows = low.astype(F32).T.astype(BF16)
    values = (total + adapter_scale_factor * dot_nn(low_rows, up_half)).astype(BF16)
    grads = []
    for g in range(KV_HEADS):
        head = values[:, g * HEAD_DIM : (g + 1) * HEAD_DIM]
        high, rest, aimed = heads[3 * g : 3 * g + 3]
        d_head = dot_nn(high[...], head) + dot_nn(rest[...], head) - aimed[...]
        grads.append(d_head.astype(BF16))
    d_values = jnp.concatenate(grads, axis=1)
    d_low_out[...] = (adapter_scale_factor * dot_nt(up_half, d_values)).astype(BF16)
    up_grad[...] = adapter_scale_factor * dot_nn(low, d_values)


def value_grads(s, n, offset, half, pieces, mine, got, up, heads, raw):
    t, u = raw[0].shape[0], raw[1].shape[0]
    return call(
        functools.partial(grad_kernel, n, offset, half),
        [((u, VALUE_WIDTH), F32), ((RANK, t), BF16), ((RANK, VALUE_WIDTH), F32)],
        s, [*raw, *pieces, mine, got, up, *[a for h in heads for a in h]],
        scratch=[pltpu.VMEM((2 * half, VALUE_WIDTH), BF16), pltpu.VMEM((RANK, 2 * half), BF16)], flops=1e9,
    )


def up_place(device, half):
    columns = VALUE_WIDTH // half
    row = pl.multiple_of(lax.div(device, columns) * UP_ROWS, UP_ROWS)
    col = lax.rem(device, columns) * half
    return pl.ds(row, UP_ROWS), lanes_at(col, half)


def down_kernel(chosen, half, s, refs, outs, scratch):
    x, xo, d_low, d_low_got, up_grad, up_got = refs
    (up_sum,) = scratch
    outs = list(outs)
    up_sum[...] = up_grad[...] + up_got[...]
    for k in chosen:
        here, packed = lanes_at((s[0] ^ k) * 2 * half + s[1] * half, half), lanes_at((s[0] ^ k) * half, half)
        part = dot_nn(d_low[...], x[:, here]) + dot_nn(d_low_got[...], xo[:, packed])
        up_piece = up_sum[up_place(s[0] ^ k, half)]
        if k == 0:
            outs.pop(0)[...] = part
            outs.pop(0)[...] = up_piece
        else:
            out = outs.pop(0)
            out[:RANK, :] = part.astype(BF16)
            out[RANK:, :] = up_piece.astype(BF16)


def down_pieces(s, chosen, half, d_low, d_low_got, up_grad, up_got, raw):
    keep = [((RANK, half), F32), ((UP_ROWS, half), F32)]
    return call(
        functools.partial(down_kernel, chosen, half),
        [o for k in chosen for o in (keep if k == 0 else [((RANK + UP_ROWS, half), BF16)])],
        s, [*raw, d_low, d_low_got, up_grad, up_got],
        scratch=[pltpu.VMEM((RANK, VALUE_WIDTH), F32)], flops=1e9,
    )


def update_kernel(s, refs, outs, scratch):
    keep, keep_up, down_ref, up_ref, *got = refs
    fresh, message = outs
    half = fresh.shape[1]
    old_down = down_ref[:, lanes_at(s[1] * half, half)]
    old_up = up_ref[up_place(s[0], half)]
    total, total_up = keep[...], keep_up[...]
    for piece in got:
        total += piece[:RANK, :].astype(F32)
        total_up += piece[RANK:, :].astype(F32)
    new_down = old_down - rate_down * total
    new_up = old_up - rate_up * total_up
    high = new_up.astype(BF16)
    fresh[...] = new_down
    message[:RANK, :] = new_down.astype(BF16)
    message[RANK : RANK + UP_ROWS, :] = high
    message[RANK + UP_ROWS :, :] = (new_up - high.astype(F32)).astype(BF16)


def update(s, keep, keep_up, down_t, up, got):
    half = keep.shape[1]
    return call(
        update_kernel,
        [((RANK, half), F32), ((RANK + 2 * UP_ROWS, half), BF16)],
        s, [keep, keep_up, down_t, up, *got],
    )


def column_kernel(n, half, s, refs, outs, scratch):
    xs, xso = refs
    (out,) = outs
    u = xs.shape[0]
    for i in range(n // 2):
        owner = 2 * i + 1 - lax.rem(s[0], 2)
        there = slice(i * half, (i + 1) * half)
        out[:u, there] = xs[:, lanes_at(owner * 2 * half + s[1] * half, half)]
        out[u:, there] = xso[:, lanes_at(owner * half, half)]


def column_rows(s, n, half, raw):
    u = raw[0].shape[0]
    return call(functools.partial(column_kernel, n, half), [((2 * u, n // 2 * half), BF16)], s, raw)[0]


def up_kernel(s, refs, outs, scratch):
    for i, message in enumerate(refs):
        place = lax.div(s[0] ^ (2 * i), 2)
        high = message[RANK : RANK + UP_ROWS, :].astype(F32)
        there = pl.ds(pl.multiple_of(place * UP_ROWS, UP_ROWS), UP_ROWS)
        outs[0][there, :] = high + message[RANK + UP_ROWS :, :].astype(F32)


def column_up(s, half, messages):
    return call(up_kernel, [((len(messages) * UP_ROWS, half), F32)], s, messages)[0]


def score_low_kernel(half, s, refs, outs, scratch):
    xs, xso, xz, *messages = refs
    mine, other, near_by, cross = outs
    u = xs.shape[0]
    sums = [0.0, 0.0, 0.0]
    for i, message in enumerate(messages):
        owner = s[0] ^ (2 * i)
        place = lax.div(owner, 2)
        down = message[:RANK, :]
        rows = (
            xs[:, lanes_at(owner * 2 * half + s[1] * half, half)],
            xso[:, lanes_at(owner * half, half)],
            xz[:, lanes_at(place * half, half)],
        )
        sums = [a + dot_nt(b, down) for a, b in zip(sums, rows)]
    mine[...] = sums[0]
    other[...] = sums[1]
    near_by[...] = sums[2][:u, :]
    cross[...] = sums[2][u:, :]


def score_low(s, half, messages, raw):
    u = raw[0].shape[0]
    return call(
        functools.partial(score_low_kernel, half),
        [((u, RANK), F32)] * 4,
        s, [*raw, *messages], flops=2e8,
    )


def score_kernel(s, refs, outs, scratch):
    base, probs, fresh, fresh_got, up, up_got, *lows = refs
    out, new_down, new_up = outs
    half = new_down.shape[1] // 2
    parity = lax.rem(s[0], 2)
    for i in range(up.shape[0] // UP_ROWS):
        rows = slice(i * UP_ROWS, (i + 1) * UP_ROWS)
        new_up[up_place(2 * i + parity, half)] = up[rows, :]
        new_up[up_place(2 * i + 1 - parity, half)] = up_got[rows, :]
    low = sum(a[...] for a in lows).astype(BF16)
    u = low.shape[0]
    values = base[...] + adapter_scale_factor * dot_nn(low, new_up[...].astype(BF16))
    values = values.astype(BF16)
    for g in range(KV_HEADS):
        attended = dot_nn(probs[g], values[:, g * HEAD_DIM : (g + 1) * HEAD_DIM]).astype(BF16)
        for j in range(GROUP):
            h = g * GROUP + j
            out[:, h * HEAD_DIM : (h + 1) * HEAD_DIM] = attended[j * u : (j + 1) * u, :]
    new_down[:, lanes_at(s[1] * half, half)] = fresh[...]
    new_down[:, lanes_at((1 - s[1]) * half, half)] = fresh_got[...]


def score(s, base, probs, fresh, fresh_got, up, up_got, lows):
    u, half = base.shape[0], fresh.shape[1]
    return call(
        score_kernel,
        [((u, Q_HEADS * HEAD_DIM), BF16), ((RANK, 2 * half), F32), ((RANK, VALUE_WIDTH), F32)],
        s, [base, probs, fresh, fresh_got, up, up_got, *lows], flops=2e8, final=(0, 1, 2),
    )


def reduce_order(n):
    far = [*range(n - 2, n // 2 - 1, -2), *range(n - 1, n // 2, -2)]
    near_by = [*range(n // 2 - 1, 0, -1)]
    return far, near_by


def solution(mesh):
    n_fsdp, n_view, n_task = mesh.shape["fsdp"], mesh.shape["view"], mesh.shape["task"]
    line = n_fsdp // 2

    def ring_device(place):
        place = place % n_fsdp
        return 2 * place if place < line else 2 * (n_fsdp - 1 - place) + 1

    forward = [(ring_device(i), ring_device(i + 1)) for i in range(n_fsdp)]
    backward = [(b, a) for a, b in forward]

    def over_view(array, bit):
        return lax.ppermute(array, "view", [(i, i ^ bit) for i in range(n_view)])

    def swap(array):
        return lax.ppermute(array, "view", [(i, i ^ 1) for i in range(n_view)])

    def exchange(array, k):
        return lax.ppermute(array, "fsdp", [(i, i ^ k) for i in range(n_fsdp)])

    def body(
        train_input,
        train_query,
        train_keys,
        train_target,
        train_segments,
        value_weight,
        adapter_down,
        adapter_up,
        score_input,
        score_query,
        score_keys,
        score_segments,
    ):
        width = train_input.shape[-1]
        x = train_input.reshape(-1, width)
        xs = score_input.reshape(-1, width)
        query, keyset, target = (a.reshape(x.shape[0], -1) for a in (train_query, train_keys, train_target))
        squery, skeyset = (a.reshape(xs.shape[0], -1) for a in (score_query, score_keys))
        shard = value_weight.shape[0]
        half = shard // 2
        me = lax.axis_index("fsdp")
        core = lax.axis_index("view") % 2
        place = jnp.where(me % 2 == 0, me // 2, n_fsdp - 1 - me // 2)
        s = jnp.stack([me, core, place, lax.axis_index("task") % 2]).astype(jnp.int32)

        down_t = adapter_down.T
        a_piece, y_piece, c_piece = prepare(value_weight, down_t)

        seg_row, sseg_row = train_segments.reshape(1, -1), score_segments.reshape(1, -1)
        near_query, near_keys, near_target = near(query), near(keyset), near(target)

        def head(g, deps):
            return train_head(s, g, seg_row, near_query, near_keys, near_target, deps)

        def onward(array, ahead):
            return lax.ppermute(array, "fsdp", forward if ahead else backward)

        def over_task(array):
            return lax.ppermute(array, "task", [(i, i ^ 1) for i in range(n_task)])

        steps = n_fsdp // 2
        arrived, offsets = [a_piece, y_piece, c_piece], [0]
        a_ahead = a_back = a_piece
        c_ahead = c_back = c_piece
        heads = [None] * KV_HEADS
        for k in range(1, steps):
            a_ahead, a_back = onward(a_ahead, True), onward(a_back, False)
            c_ahead, c_back = onward(c_ahead, True), onward(c_back, False)
            if k == 1:
                xo, xso = fetch(s, n_fsdp, half, (x, xs))
                xo, xso = swap(xo), swap(xso)
                raw = tuple(near(a) for a in (x, xo, xs, xso))
                touched = touch(s, (near_query, near_keys, near_target, seg_row))[0]
                heads[0] = head(0, (touched,))
                probs = score_probs(s, sseg_row, squery, skeyset, ())
            elif k == 2:
                heads[1] = head(1, ())
                heads[2] = head(2, ())
            elif k == 3:
                partial = project(s, n_fsdp, offsets, half, arrived, (), raw, False)
                cut = len(offsets)
            arrived += [a_ahead, over_task(a_ahead), c_ahead]
            arrived += [a_back, over_task(a_back), c_back]
            offsets += [n_fsdp - k, k]
        a_last, c_last = onward(a_ahead, True), onward(c_back, False)
        last = [a_last, over_task(a_last), c_last]
        heads[3] = head(3, ())
        sums, sums_out = project(s, n_fsdp, offsets[cut:], half, arrived[3 * cut :], partial, raw, True)
        sums_got = swap(sums_out)
        last += [swap(a) for a in last]
        base, d_low, up_grad = value_grads(
            s, n_fsdp, steps, half, last, sums, sums_got, adapter_up, heads, (raw[0], raw[2])
        )
        d_low_got, up_got = swap(d_low), swap(up_grad)
        far, near_by = reduce_order(n_fsdp)
        out = [None] * (n_fsdp - 1)

        def pieces_of(chosen):
            return down_pieces(s, chosen, half, d_low, d_low_got, up_grad, up_got, raw[:2])

        for k, array in zip(far, pieces_of(far)):
            out[k - 1] = array
        *some, keep, keep_up = pieces_of([*near_by, 0])
        for k, array in zip(near_by, some):
            out[k - 1] = array
        bit = 2
        while bit < n_view:
            keep, keep_up = (a + over_view(a, bit) for a in (keep, keep_up))
            out = [(a.astype(F32) + over_view(a, bit).astype(F32)).astype(BF16) for a in out]
            bit *= 2

        got = [None] * len(out)
        for k in far + near_by:
            got[k - 1] = exchange(out[k - 1], k)
        fresh, message = update(s, keep, keep_up, down_t, adapter_up, got)
        xz = exchange(column_rows(s, n_fsdp, half, raw[2:]), 1)
        messages = [message] + [None] * (n_fsdp // 2 - 1)
        for k in range(n_fsdp - 2, 0, -2):
            messages[k // 2] = exchange(message, k)
        fresh_got = swap(fresh)
        up = column_up(s, half, messages)
        up_got = exchange(up, 1)
        low, other, near_by, cross = score_low(s, half, messages, [*raw[2:], xz])
        pairs = [
            (i * n_view + v, (i ^ 1) * n_view + (v ^ 1)) for i in range(n_fsdp) for v in range(n_view)
        ]
        lows = [low, exchange(near_by, 1), lax.ppermute(cross, ("fsdp", "view"), pairs), swap(other)]
        scored, new_down, new_up = score(s, base, probs, fresh, fresh_got, up, up_got, lows)
        return (new_down.T, new_up, scored.reshape(score_query.shape))

    rows, rank_rows, tasks = P(("task", "view"), "fsdp", None), P(("task", "fsdp"), None), P("task", None)
    in_specs = (*[rows] * 5, P("fsdp", None), rank_rows, tasks, *[rows] * 4)
    out_specs = (rank_rows, tasks, rows)
    return jax.shard_map(body, mesh=mesh, in_specs=in_specs, out_specs=out_specs, check_vma=False)
```

```python
import functools

import jax
import jax.numpy as jnp
from jax import lax
from jax.experimental import pallas as pl
from jax.experimental.pallas import tpu as pltpu
from jax.sharding import PartitionSpec as P


Q_HEADS = 32
KV_HEADS = 4
HEAD_DIM = 128
GROUP = 8
VALUE_WIDTH = 512
RANK = 64
UP_ROWS = 8

adapter_scale_factor = 0.5
rate_down = 2e-05
rate_up = 0.001


F32 = jnp.float32
BF16 = jnp.bfloat16
VM = pl.BlockSpec(memory_space=pltpu.VMEM)
SM = pl.BlockSpec(memory_space=pltpu.SMEM)
ANY = pl.BlockSpec(memory_space=pl.ANY)
HBM = pl.BlockSpec(memory_space=pltpu.MemorySpace.HBM)
VMEM_GRANT = 16 * 2**20


def dot_nn(a, b):
    return lax.dot_general(a, b, (((1,), (0,)), ((), ())), preferred_element_type=F32)


def dot_nt(a, b):
    return lax.dot_general(a, b, (((1,), (1,)), ((), ())), preferred_element_type=F32)


def cost(flops, nbytes):
    return pl.CostEstimate(flops=int(flops), bytes_accessed=int(nbytes), transcendentals=0)


def near(array):
    return pltpu.with_memory_space_constraint(array, pltpu.VMEM)


def far_off(array):
    return pltpu.with_memory_space_constraint(array, pltpu.MemorySpace.HBM)


def call(kernel, outs, scalars, operands, scratch=(), flops=1e6, final=(), deps=()):
    n, d = len(operands), len(deps)

    def whole(scalar_ref, *refs):
        kernel(scalar_ref, refs[:n], refs[n + d : n + d + len(outs)], refs[n + d + len(outs) :])

    return pl.pallas_call(
        whole,
        out_shape=[jax.ShapeDtypeStruct(*o) if i in final else pltpu.VMEM(*o) for i, o in enumerate(outs)],
        in_specs=[SM] + [VM] * n + [ANY] * d,
        out_specs=[VM] * len(outs),
        scratch_shapes=list(scratch),
        cost_estimate=cost(flops, 2**20),
        compiler_params=pltpu.CompilerParams(vmem_limit_bytes=VMEM_GRANT),
    )(scalars, *[near(a) for a in operands], *deps)


def lanes_at(start, size):
    return pl.ds(pl.multiple_of(start, 128), size)


def same_segment(seg_row):
    length = seg_row.shape[1]
    across = jnp.broadcast_to(seg_row[...].astype(F32), (length, length))
    return across == across.T


def train_heads_kernel(some, s, refs, outs, scratch):
    seg_row, q_ref, k_ref, t_ref = refs
    length = k_ref.shape[0]
    row = lax.broadcasted_iota(jnp.int32, (length, length), 0)
    col = lax.broadcasted_iota(jnp.int32, (length, length), 1)
    allowed = (row <= col) & same_segment(seg_row)
    for i, g in enumerate(some):
        high_out, rest_out, aimed_out = outs[3 * i : 3 * i + 3]
        keys = k_ref[:, g * HEAD_DIM : (g + 1) * HEAD_DIM]
        lanes = [slice(h * HEAD_DIM, (h + 1) * HEAD_DIM) for h in range(g * GROUP, (g + 1) * GROUP)]
        every = []
        for j in range(GROUP):
            logits = dot_nt(keys, q_ref[:, lanes[j]]) * HEAD_DIM ** (-0.5)
            logits = jnp.where(allowed, logits, -1e30)
            peak = jnp.max(logits, axis=0, keepdims=True)
            weights = jnp.exp(logits - peak)
            every.append((weights * (1.0 / jnp.sum(weights, axis=0, keepdims=True))).astype(BF16))
        gram = sum(dot_nt(probs, probs) for probs in every)
        high = gram.astype(BF16)
        high_out[...] = high
        rest_out[...] = (gram - high.astype(F32)).astype(BF16)
        aimed_out[...] = sum(dot_nn(probs, t_ref[:, lanes[j]]) for j, probs in enumerate(every))


def train_heads(s, some, seg_row, query, keyset, target):
    length = query.shape[0]
    got = call(
        functools.partial(train_heads_kernel, some),
        [((length, length), BF16), ((length, length), BF16), ((length, HEAD_DIM), F32)] * len(some),
        s, [seg_row, query, keyset, target], flops=2e9,
    )
    return [got[3 * i : 3 * i + 3] for i in range(len(some))]


def score_probs_kernel(s, refs, outs, scratch):
    seg_row, q_ref, k_ref = refs
    (p_ref,) = outs
    length = k_ref.shape[0]
    row = lax.broadcasted_iota(jnp.int32, (length, length), 0)
    col = lax.broadcasted_iota(jnp.int32, (length, length), 1)
    allowed = (col <= row) & same_segment(seg_row)
    for g in range(KV_HEADS):
        keys = k_ref[:, g * HEAD_DIM : (g + 1) * HEAD_DIM]
        for j in range(GROUP):
            h = g * GROUP + j
            logits = dot_nt(q_ref[:, h * HEAD_DIM : (h + 1) * HEAD_DIM], keys) * HEAD_DIM ** (-0.5)
            logits = jnp.where(allowed, logits, -1e30)
            weights = jnp.exp(logits - jnp.max(logits, axis=1, keepdims=True))
            probs = weights / jnp.sum(weights, axis=1, keepdims=True)
            p_ref[g, j * length : (j + 1) * length, :] = probs.astype(BF16)


def score_probs(s, seg_row, query, keyset, deps):
    length = query.shape[0]
    return call(
        score_probs_kernel, [((KV_HEADS, GROUP * length, length), BF16)],
        s, [seg_row, query, keyset], flops=1e9, deps=deps,
    )[0]


def apart(half):
    return half * 5 // 16


def unpack_down(packed, half):
    parts = VALUE_WIDTH // half
    if parts == 1:
        return packed
    return jnp.concatenate([packed[:, i * half : (i + 1) * half] for i in range(parts)], axis=0)


def pack_down(block, half):
    parts = VALUE_WIDTH // half
    if parts == 1:
        return block
    rows = block.shape[0] // parts
    return jnp.concatenate([block[i * rows : (i + 1) * rows] for i in range(parts)], axis=1)


def assemble(s, half, a, y, c, buffer):
    rows = apart(half)
    buffer[pl.ds(pl.multiple_of(s[3] * rows, 16), rows), :] = a[...]
    buffer[pl.ds(pl.multiple_of((1 - s[3]) * rows, 16), rows), :] = y[...]
    buffer[2 * rows :, :] = c[: half - 2 * rows, :]
    return unpack_down(c[half - 2 * rows :, :], half)


def prepare_kernel(half, w_hbm, d_hbm, a, y, c, down, sems):
    core, task = lax.axis_index("view") % 2, lax.axis_index("task") % 2
    rows = apart(half)
    rest = half - 2 * rows

    def weight_rows(start, count):
        return w_hbm.at[pl.ds(pl.multiple_of(core * half + start, 16), count), :]

    copies = [
        pltpu.make_async_copy(weight_rows(task * rows, rows), a, sems.at[0]),
        pltpu.make_async_copy(weight_rows((1 - task) * rows, rows), y, sems.at[1]),
        pltpu.make_async_copy(weight_rows(2 * rows, rest), c.at[pl.ds(0, rest), :], sems.at[2]),
        pltpu.make_async_copy(d_hbm.at[:, lanes_at(core * half, half)], down, sems.at[3]),
    ]
    for copy in copies:
        copy.start()
    copies[3].wait()
    c[rest:, :] = pack_down(down[...].astype(BF16), half)
    for copy in copies[:3]:
        copy.wait()


def prepare(weight, down_t):
    half = weight.shape[0] // 2
    rows = apart(half)
    sizes = (rows, rows, half - 2 * rows + RANK * half // VALUE_WIDTH)
    return pl.pallas_call(
        functools.partial(prepare_kernel, half),
        out_shape=[pltpu.VMEM((size, VALUE_WIDTH), BF16) for size in sizes],
        in_specs=[HBM, HBM],
        out_specs=[VM] * 3,
        scratch_shapes=[pltpu.VMEM((RANK, half), F32), pltpu.SemaphoreType.DMA((4,))],
        cost_estimate=cost(1e6, 2**20),
        compiler_params=pltpu.CompilerParams(vmem_limit_bytes=VMEM_GRANT),
    )(far_off(weight), far_off(down_t))


def owner_of(position, n):
    position = lax.rem(position, n)
    return jnp.where(position < n // 2, 2 * position, 2 * (n - 1 - position) + 1)


def fetch_kernel(n, half, s, refs, outs, scratch):
    (sems,) = scratch
    copies = []
    for i, (source, out) in enumerate(zip(refs, outs)):
        for j in range(n):
            here = lanes_at(2 * half * j + (1 - s[1]) * half, half)
            copies.append(
                pltpu.make_async_copy(source.at[:, here], out.at[:, pl.ds(j * half, half)], sems.at[i * n + j])
            )
    for copy in copies:
        copy.start()
    for copy in copies:
        copy.wait()


def fetch(s, n, half, arrays):
    def kernel(scalar_ref, *refs):
        m = len(arrays)
        fetch_kernel(n, half, scalar_ref, refs[:m], refs[m : 2 * m], refs[2 * m :])

    return pl.pallas_call(
        kernel,
        out_shape=[pltpu.VMEM((a.shape[0], n * half), BF16) for a in arrays],
        in_specs=[SM] + [HBM] * len(arrays),
        out_specs=[VM] * len(arrays),
        scratch_shapes=[pltpu.SemaphoreType.DMA((len(arrays) * n,))],
        cost_estimate=cost(1e6, 2**21),
        compiler_params=pltpu.CompilerParams(vmem_limit_bytes=VMEM_GRANT),
    )(s, *[far_off(a) for a in arrays])


def project_kernel(n, offsets, half, s, refs, outs, scratch):
    x, xo, xs, xso = refs[:4]
    refs = refs[4:]
    xb, wb, db = scratch
    t, u = x.shape[0], xs.shape[0]
    for i, offset in enumerate(offsets):
        owner = owner_of(s[2] + offset, n)
        whole, packed = lanes_at(owner * 2 * half + s[1] * half, half), lanes_at(owner * half, half)
        there = slice(i * half, (i + 1) * half)
        for at, a, here in ((0, x, whole), (t, xo, packed), (2 * t, xs, whole), (2 * t + u, xso, packed)):
            xb[at : at + a.shape[0], there] = a[:, here]
        db[:, there] = assemble(s, half, *refs[3 * i : 3 * i + 3], wb.at[pl.ds(i * half, half), :])
    total = dot_nn(xb[...], wb[...])
    low = dot_nt(db[...], xb[: 2 * t, :])
    before = refs[3 * len(offsets) :]
    if before:
        total = total + before[0][...]
        low = low + before[1][...]
    if outs[0].shape[0] == total.shape[0]:
        outs[0][...] = total
        outs[1][...] = low
        return
    for i, out in enumerate(outs):
        out[:t, :] = total[i * t : (i + 1) * t, :]
        out[t : t + u, :] = total[2 * t + i * u : 2 * t + (i + 1) * u, :]
        part = low[:, i * t : (i + 1) * t]
        out[t + u :, :t] = part[: RANK // 2, :]
        out[t + u :, t : 2 * t] = part[RANK // 2 :, :]


def project(s, n, offsets, half, pieces, before, raw, final):
    t, u = raw[0].shape[0], raw[2].shape[0]
    if final:
        outs = [((t + u + RANK // 2, VALUE_WIDTH), F32)] * 2
    else:
        outs = [((2 * t + 2 * u, VALUE_WIDTH), F32), ((RANK, 2 * t), F32)]
    return call(
        functools.partial(project_kernel, n, offsets, half),
        outs, s, [*raw, *pieces, *before],
        scratch=[
            pltpu.VMEM((2 * t + 2 * u, len(offsets) * half), BF16),
            pltpu.VMEM((len(offsets) * half, VALUE_WIDTH), BF16),
            pltpu.VMEM((RANK, len(offsets) * half), BF16),
        ],
        flops=len(offsets) * 3.4e8,
    )


def grad_kernel(n, offset, half, s, refs, outs, scratch):
    x, xs = refs[:2]
    pieces, (mine, got, up_ref), heads = refs[2:8], refs[8:11], refs[11:]
    base, d_low_out, up_grad = outs
    wb, db = scratch
    t, u = x.shape[0], xs.shape[0]
    total = mine[:t, :] + got[:t, :]
    base_total = mine[t : t + u, :] + got[t : t + u, :]
    packed = mine[t + u :, :] + got[t + u :, :]
    low = jnp.concatenate([packed[:, :t], packed[:, t : 2 * t]], axis=0)
    for i in range(2):
        start = pl.multiple_of((s[1] if i == 0 else 1 - s[1]) * half, half)
        db[:, lanes_at(start, half)] = assemble(s, half, *pieces[3 * i : 3 * i + 3], wb.at[pl.ds(start, half), :])
    here = lanes_at(owner_of(s[2] + offset, n) * 2 * half, 2 * half)
    total = total + dot_nn(x[:, here], wb[...])
    base_total = base_total + dot_nn(xs[:, here], wb[...])
    low = low + dot_nt(db[...], x[:, here])
    base[...] = base_total
    low = low.astype(BF16)
    up_half = up_ref[...].astype(BF16)
    low_rows = low.astype(F32).T.astype(BF16)
    values = (total + adapter_scale_factor * dot_nn(low_rows, up_half)).astype(BF16)
    grads = []
    for g in range(KV_HEADS):
        head = values[:, g * HEAD_DIM : (g + 1) * HEAD_DIM]
        high, rest, aimed = heads[3 * g : 3 * g + 3]
        d_head = dot_nn(high[...], head) + dot_nn(rest[...], head) - aimed[...]
        grads.append(d_head.astype(BF16))
    d_values = jnp.concatenate(grads, axis=1)
    d_low_out[...] = (adapter_scale_factor * dot_nt(up_half, d_values)).astype(BF16)
    up_grad[...] = adapter_scale_factor * dot_nn(low, d_values)


def value_grads(s, n, offset, half, pieces, mine, got, up, heads, raw):
    t, u = raw[0].shape[0], raw[1].shape[0]
    return call(
        functools.partial(grad_kernel, n, offset, half),
        [((u, VALUE_WIDTH), F32), ((RANK, t), BF16), ((RANK, VALUE_WIDTH), F32)],
        s, [*raw, *pieces, mine, got, up, *[a for h in heads for a in h]],
        scratch=[pltpu.VMEM((2 * half, VALUE_WIDTH), BF16), pltpu.VMEM((RANK, 2 * half), BF16)], flops=1e9,
    )


def up_place(device, half):
    columns = VALUE_WIDTH // half
    row = pl.multiple_of(lax.div(device, columns) * UP_ROWS, UP_ROWS)
    col = lax.rem(device, columns) * half
    return pl.ds(row, UP_ROWS), lanes_at(col, half)


def down_kernel(chosen, half, s, refs, outs, scratch):
    x, xo, d_low, d_low_got, up_grad, up_got = refs
    (up_sum,) = scratch
    outs = list(outs)
    up_sum[...] = up_grad[...] + up_got[...]
    for k in chosen:
        here, packed = lanes_at((s[0] ^ k) * 2 * half + s[1] * half, half), lanes_at((s[0] ^ k) * half, half)
        part = dot_nn(d_low[...], x[:, here]) + dot_nn(d_low_got[...], xo[:, packed])
        up_piece = up_sum[up_place(s[0] ^ k, half)]
        if k == 0:
            outs.pop(0)[...] = part
            outs.pop(0)[...] = up_piece
        else:
            out = outs.pop(0)
            out[:RANK, :] = part.astype(BF16)
            out[RANK:, :] = up_piece.astype(BF16)


def down_pieces(s, chosen, half, d_low, d_low_got, up_grad, up_got, raw):
    keep = [((RANK, half), F32), ((UP_ROWS, half), F32)]
    return call(
        functools.partial(down_kernel, chosen, half),
        [o for k in chosen for o in (keep if k == 0 else [((RANK + UP_ROWS, half), BF16)])],
        s, [*raw, d_low, d_low_got, up_grad, up_got],
        scratch=[pltpu.VMEM((RANK, VALUE_WIDTH), F32)], flops=1e9,
    )


def update_kernel(s, refs, outs, scratch):
    keep, keep_up, down_ref, up_ref, *got = refs
    fresh, message = outs
    half = fresh.shape[1]
    old_down = down_ref[:, lanes_at(s[1] * half, half)]
    old_up = up_ref[up_place(s[0], half)]
    total, total_up = keep[...], keep_up[...]
    for piece in got:
        total += piece[:RANK, :].astype(F32)
        total_up += piece[RANK:, :].astype(F32)
    new_down = old_down - rate_down * total
    new_up = old_up - rate_up * total_up
    high = new_up.astype(BF16)
    fresh[...] = new_down
    message[:RANK, :] = new_down.astype(BF16)
    message[RANK : RANK + UP_ROWS, :] = high
    message[RANK + UP_ROWS :, :] = (new_up - high.astype(F32)).astype(BF16)


def update(s, keep, keep_up, down_t, up, got):
    half = keep.shape[1]
    return call(
        update_kernel,
        [((RANK, half), F32), ((RANK + 2 * UP_ROWS, half), BF16)],
        s, [keep, keep_up, down_t, up, *got],
    )


def column_kernel(n, half, s, refs, outs, scratch):
    xs, xso = refs
    (out,) = outs
    u = xs.shape[0]
    for i in range(n // 2):
        owner = 2 * i + 1 - lax.rem(s[0], 2)
        there = slice(i * half, (i + 1) * half)
        out[:u, there] = xs[:, lanes_at(owner * 2 * half + s[1] * half, half)]
        out[u:, there] = xso[:, lanes_at(owner * half, half)]


def column_rows(s, n, half, raw):
    u = raw[0].shape[0]
    return call(functools.partial(column_kernel, n, half), [((2 * u, n // 2 * half), BF16)], s, raw)[0]


def up_kernel(s, refs, outs, scratch):
    for i, message in enumerate(refs):
        place = lax.div(s[0] ^ (2 * i), 2)
        high = message[RANK : RANK + UP_ROWS, :].astype(F32)
        there = pl.ds(pl.multiple_of(place * UP_ROWS, UP_ROWS), UP_ROWS)
        outs[0][there, :] = high + message[RANK + UP_ROWS :, :].astype(F32)


def column_up(s, half, messages):
    return call(up_kernel, [((len(messages) * UP_ROWS, half), F32)], s, messages)[0]


def score_low_kernel(half, s, refs, outs, scratch):
    xs, xso, xz, *messages = refs
    mine, other, near_by, cross = outs
    u = xs.shape[0]
    sums = [0.0, 0.0, 0.0]
    for i, message in enumerate(messages):
        owner = s[0] ^ (2 * i)
        place = lax.div(owner, 2)
        down = message[:RANK, :]
        rows = (
            xs[:, lanes_at(owner * 2 * half + s[1] * half, half)],
            xso[:, lanes_at(owner * half, half)],
            xz[:, lanes_at(place * half, half)],
        )
        sums = [a + dot_nt(b, down) for a, b in zip(sums, rows)]
    mine[...] = sums[0]
    other[...] = sums[1]
    near_by[...] = sums[2][:u, :]
    cross[...] = sums[2][u:, :]


def score_low(s, half, messages, raw):
    u = raw[0].shape[0]
    return call(
        functools.partial(score_low_kernel, half),
        [((u, RANK), F32)] * 4,
        s, [*raw, *messages], flops=2e8,
    )


def renew_kernel(s, refs, outs, scratch):
    fresh, fresh_got, up, up_got = refs
    new_down, new_up, kept_up = outs
    half = new_down.shape[1] // 2
    parity = lax.rem(s[0], 2)
    for i in range(up.shape[0] // UP_ROWS):
        rows = slice(i * UP_ROWS, (i + 1) * UP_ROWS)
        new_up[up_place(2 * i + parity, half)] = up[rows, :]
        new_up[up_place(2 * i + 1 - parity, half)] = up_got[rows, :]
    new_down[:, lanes_at(s[1] * half, half)] = fresh[...]
    new_down[:, lanes_at((1 - s[1]) * half, half)] = fresh_got[...]
    kept_up[...] = new_up[...]


def renew(s, fresh, fresh_got, up, up_got):
    half = fresh.shape[1]
    return call(
        renew_kernel, [((RANK, 2 * half), F32)] + [((RANK, VALUE_WIDTH), F32)] * 2,
        s, [fresh, fresh_got, up, up_got], final=(0, 1),
    )


def score_kernel(s, refs, outs, scratch):
    base, probs, new_up, *lows = refs
    (out,) = outs
    low = sum(a[...] for a in lows).astype(BF16)
    u = low.shape[0]
    values = base[...] + adapter_scale_factor * dot_nn(low, new_up[...].astype(BF16))
    values = values.astype(BF16)
    for g in range(KV_HEADS):
        attended = dot_nn(probs[g], values[:, g * HEAD_DIM : (g + 1) * HEAD_DIM]).astype(BF16)
        for j in range(GROUP):
            h = g * GROUP + j
            out[:, h * HEAD_DIM : (h + 1) * HEAD_DIM] = attended[j * u : (j + 1) * u, :]


def score(s, base, probs, new_up, lows):
    return call(
        score_kernel, [((base.shape[0], Q_HEADS * HEAD_DIM), BF16)], s, [base, probs, new_up, *lows],
        flops=2e8, final=(0,),
    )[0]


def reduce_order(n):
    far = [*range(n - 2, n // 2 - 1, -2), *range(n - 1, n // 2, -2)]
    near_by = [*range(n // 2 - 1, 0, -1)]
    return far, near_by


def solution(mesh):
    n_fsdp, n_view, n_task = mesh.shape["fsdp"], mesh.shape["view"], mesh.shape["task"]
    line = n_fsdp // 2

    def ring_device(place):
        place = place % n_fsdp
        return 2 * place if place < line else 2 * (n_fsdp - 1 - place) + 1

    forward = [(ring_device(i), ring_device(i + 1)) for i in range(n_fsdp)]
    backward = [(b, a) for a, b in forward]

    def over_view(array, bit):
        return lax.ppermute(array, "view", [(i, i ^ bit) for i in range(n_view)])

    def swap(array):
        return lax.ppermute(array, "view", [(i, i ^ 1) for i in range(n_view)])

    def exchange(array, k):
        return lax.ppermute(array, "fsdp", [(i, i ^ k) for i in range(n_fsdp)])

    def body(
        train_input,
        train_query,
        train_keys,
        train_target,
        train_segments,
        value_weight,
        adapter_down,
        adapter_up,
        score_input,
        score_query,
        score_keys,
        score_segments,
    ):
        width = train_input.shape[-1]
        x = train_input.reshape(-1, width)
        xs = score_input.reshape(-1, width)
        query, keyset, target = (a.reshape(x.shape[0], -1) for a in (train_query, train_keys, train_target))
        squery, skeyset = (a.reshape(xs.shape[0], -1) for a in (score_query, score_keys))
        shard = value_weight.shape[0]
        half = shard // 2
        me = lax.axis_index("fsdp")
        core = lax.axis_index("view") % 2
        place = jnp.where(me % 2 == 0, me // 2, n_fsdp - 1 - me // 2)
        s = jnp.stack([me, core, place, lax.axis_index("task") % 2]).astype(jnp.int32)

        down_t = adapter_down.T
        a_piece, y_piece, c_piece = prepare(value_weight, down_t)

        seg_row, sseg_row = train_segments.reshape(1, -1), score_segments.reshape(1, -1)
        near_query, near_keys, near_target = near(query), near(keyset), near(target)

        def head_pair(some):
            return train_heads(s, some, seg_row, near_query, near_keys, near_target)

        def onward(array, ahead):
            return lax.ppermute(array, "fsdp", forward if ahead else backward)

        def over_task(array):
            return lax.ppermute(array, "task", [(i, i ^ 1) for i in range(n_task)])

        steps = n_fsdp // 2
        arrived, offsets = [a_piece, y_piece, c_piece], [0]
        a_ahead = a_back = a_piece
        c_ahead = c_back = c_piece
        for k in range(1, steps):
            a_ahead, a_back = onward(a_ahead, True), onward(a_back, False)
            c_ahead, c_back = onward(c_ahead, True), onward(c_back, False)
            if k == 1:
                xo, xso = fetch(s, n_fsdp, half, (x, xs))
                xo, xso = swap(xo), swap(xso)
                raw = tuple(near(a) for a in (x, xo, xs, xso))
                heads = head_pair((0, 1)) + head_pair((2, 3))
                probs = score_probs(s, sseg_row, squery, skeyset, ())
            elif k == 3:
                partial = project(s, n_fsdp, offsets, half, arrived, (), raw, False)
                cut = len(offsets)
            arrived += [a_ahead, over_task(a_ahead), c_ahead]
            arrived += [a_back, over_task(a_back), c_back]
            offsets += [n_fsdp - k, k]
        a_last, c_last = onward(a_ahead, True), onward(c_back, False)
        last = [a_last, over_task(a_last), c_last]
        sums, sums_out = project(s, n_fsdp, offsets[cut:], half, arrived[3 * cut :], partial, raw, True)
        sums_got = swap(sums_out)
        last += [swap(a) for a in last]
        base, d_low, up_grad = value_grads(
            s, n_fsdp, steps, half, last, sums, sums_got, adapter_up, heads, (raw[0], raw[2])
        )
        d_low_got, up_got = swap(d_low), swap(up_grad)
        far, near_by = reduce_order(n_fsdp)
        out = [None] * (n_fsdp - 1)

        def pieces_of(chosen):
            return down_pieces(s, chosen, half, d_low, d_low_got, up_grad, up_got, raw[:2])

        for k, array in zip(far, pieces_of(far)):
            out[k - 1] = array
        *some, keep, keep_up = pieces_of([*near_by, 0])
        for k, array in zip(near_by, some):
            out[k - 1] = array
        bit = 2
        while bit < n_view:
            keep, keep_up = (a + over_view(a, bit) for a in (keep, keep_up))
            out = [(a.astype(F32) + over_view(a, bit).astype(F32)).astype(BF16) for a in out]
            bit *= 2

        got = [None] * len(out)
        for k in far + near_by:
            got[k - 1] = exchange(out[k - 1], k)
        fresh, message = update(s, keep, keep_up, down_t, adapter_up, got)
        xz = exchange(column_rows(s, n_fsdp, half, raw[2:]), 1)
        messages = [message] + [None] * (n_fsdp // 2 - 1)
        for k in range(n_fsdp - 2, 0, -2):
            messages[k // 2] = exchange(message, k)
        fresh_got = swap(fresh)
        up = column_up(s, half, messages)
        up_got = exchange(up, 1)
        low, other, near_by, cross = score_low(s, half, messages, [*raw[2:], xz])
        pairs = [
            (i * n_view + v, (i ^ 1) * n_view + (v ^ 1)) for i in range(n_fsdp) for v in range(n_view)
        ]
        lows = [low, exchange(near_by, 1), lax.ppermute(cross, ("fsdp", "view"), pairs), swap(other)]
        new_down, new_up, kept_up = renew(s, fresh, fresh_got, up, up_got)
        scored = score(s, base, probs, kept_up, lows)
        return (new_down.T, new_up, scored.reshape(score_query.shape))

    rows, rank_rows, tasks = P(("task", "view"), "fsdp", None), P(("task", "fsdp"), None), P("task", None)
    in_specs = (*[rows] * 5, P("fsdp", None), rank_rows, tasks, *[rows] * 4)
    out_specs = (rank_rows, tasks, rows)
    return jax.shard_map(body, mesh=mesh, in_specs=in_specs, out_specs=out_specs, check_vma=False)
```
